32 devices in a mesh: clips: 2 (over y), frame: 4 (over z), rows: 2 (over x), view: 2 (over core).
Axes of the slice: x: 2, y: 2, z: 4, core: 2. Of those that a mesh axis runs over, the one named last changes fastest.
Arguments:
- feats: bfloat16 [4, 4, 8, 480, 256], P(('clips', 'view'), 'frame', 'rows'), parts along dimension 0, may hold values from -8 to 8
- norm_gains: float32 [3, 256], replicated, may hold values from 0.6 to 10
- cross_qkv: bfloat16 [256, 768], replicated, may hold values from -0.45 to 0.45
- cross_out: bfloat16 [256, 256], replicated, may hold values from -0.375 to 0.375
- time_qkv: bfloat16 [256, 768], replicated, may hold values from -0.45 to 0.45
- time_out: bfloat16 [256, 256], replicated, may hold values from -0.375 to 0.375
- mlp_in: bfloat16 [256, 1024], replicated, may hold values from -0.375 to 0.375
- mlp_out: bfloat16 [1024, 256], replicated, may hold values from -0.1875 to 0.1875
Outputs:
- result: bfloat16 [4, 4, 8, 480, 256], P(('clips', 'view'), 'frame', 'rows'), parts along dimension 0
The draws below stay inside these ranges and needn't reach their ends.
There are 2 independent parts, one for each index of `clips`. The reference program is written for one: setup_inputs(seed, part) draws one part's arguments, and reference() takes and returns one part's arrays. A program takes and returns all parts, laid end to end along the dimension named above; an argument that names none is the same for every part. Nothing has to cross between parts.
All inputs are finite; a program needn't handle non-finite values.
Results may differ from the reference program's by a relative error of at most 0.012.
Values may be sent and summed in bfloat16 or wider, within the bound.
No kernel may reach another device: no remote copies, remote signals or barrier semaphores. Data moves between devices by JAX's collectives and lax.ppermute only.
A program may use at most 64 MiB of HBM per device.

```python
import jax
import jax.numpy as jnp
from jax import lax

C = 256
HEADS = 8
FFN = 1024
W = 480
FRAMES = 4
H = 8


def draw_feats(key, part):
    subkeys = jax.random.split(key, 6)
    return jnp.clip(jax.random.normal(subkeys[5], (2, FRAMES, H, W, C), jnp.float32), -6.0, 6.0).astype(jnp.bfloat16)


def tied_weight(key):
    weight = jnp.clip(jax.random.normal(key, (C, 3 * C), jnp.float32), -6.0, 6.0) * C ** (-0.5)
    return jnp.clip(weight, -0.45, 0.45)


def draw_cross_qkv(key, part):
    return tied_weight(jax.random.fold_in(key, 11)).astype(jnp.bfloat16)


def draw_time_qkv(key, part):
    return tied_weight(jax.random.fold_in(key, 23)).astype(jnp.bfloat16)


def draw_norm_gains(key, part):
    subkeys = jax.random.split(key, 1)
    drawn = jax.random.uniform(subkeys[0], (3, C), jnp.float32, 0.6, 1.4)
    return drawn


def bell_draw(key, shape, scale, most, held_as=jnp.bfloat16):
    return jnp.clip(scale * jax.random.normal(key, shape, jnp.float32), -most, most).astype(held_as)


def setup_inputs(seed: int = 0, part: int = 0) -> dict:
    arg_keys = jax.random.split(jax.random.key(seed), 9)
    own_keys = jax.random.split(jax.random.fold_in(arg_keys[8], part), 9)
    return {
        "feats": draw_feats(jax.random.fold_in(jax.random.fold_in(arg_keys[8], part), 71), part),
        "norm_gains": draw_norm_gains(jax.random.fold_in(arg_keys[8], 71), part),
        "cross_qkv": draw_cross_qkv(jax.random.fold_in(arg_keys[8], 71), part),
        "cross_out": bell_draw(arg_keys[3], (C, C), C ** -0.5, 0.375),
        "time_qkv": draw_time_qkv(jax.random.fold_in(arg_keys[8], 71), part),
        "time_out": bell_draw(arg_keys[5], (C, C), C ** -0.5, 0.375),
        "mlp_in": bell_draw(arg_keys[6], (C, FFN), C ** -0.5, 0.375),
        "mlp_out": bell_draw(arg_keys[7], (FFN, C), FFN ** -0.5, 0.1875),
    }


EPSILON = 1e-05

def layer_norm(values, norm_gain):
    wide = values.astype(jnp.float32)
    centre = lax.optimization_barrier(jnp.mean(wide, axis=-1, keepdims=True))
    spread = lax.optimization_barrier(jnp.mean((wide - centre) ** 2, axis=-1, keepdims=True))
    return ((wide - centre) * lax.rsqrt(spread + EPSILON) * norm_gain).astype(jnp.bfloat16)

def row_attend(queries, key_rows, value_rows):
    length, channels = queries.shape
    head_dim = channels // HEADS
    q_heads = queries.astype(jnp.float32).reshape(length, HEADS, head_dim)
    k_heads = key_rows.astype(jnp.float32).reshape(length, HEADS, head_dim)
    v_heads = value_rows.astype(jnp.float32).reshape(length, HEADS, head_dim)
    scores = jnp.einsum('qhd,khd->hqk', q_heads, k_heads) * head_dim ** (-0.5)
    top_score = lax.optimization_barrier(jnp.max(scores, axis=-1, keepdims=True))
    expo = jnp.exp(scores - top_score)
    shares = (expo / lax.optimization_barrier(jnp.sum(expo, axis=-1, keepdims=True))).astype(jnp.bfloat16)
    mixed = jnp.einsum('hqk,khd->qhd', shares.astype(jnp.float32), v_heads)
    return mixed.reshape(length, channels).astype(jnp.bfloat16)

def time_attend(queries, key_rows, value_rows):
    frames, pixels, channels = queries.shape
    head_dim = channels // HEADS
    q_heads = queries.astype(jnp.float32).reshape(frames, pixels, HEADS, head_dim)
    k_heads = key_rows.astype(jnp.float32).reshape(frames, pixels, HEADS, head_dim)
    v_heads = value_rows.astype(jnp.float32).reshape(frames, pixels, HEADS, head_dim)
    scores = jnp.einsum('fnhd,gnhd->hfgn', q_heads, k_heads) * head_dim ** (-0.5)
    top_score = lax.optimization_barrier(jnp.max(scores, axis=2, keepdims=True))
    expo = jnp.exp(scores - top_score)
    shares = (expo / lax.optimization_barrier(jnp.sum(expo, axis=2, keepdims=True))).astype(jnp.bfloat16)
    mixed = jnp.einsum('hfgn,gnhd->fnhd', shares.astype(jnp.float32), v_heads)
    return mixed.reshape(frames, pixels, channels).astype(jnp.bfloat16)

def reference(feats, norm_gains, cross_qkv, cross_out, time_qkv, time_out, mlp_in, mlp_out):
    views, frames, height, row_width, channels = feats.shape
    tokens_flat = feats.reshape(-1, channels)
    normed_a = layer_norm(tokens_flat, norm_gains[0])
    projected = jnp.dot(normed_a, cross_qkv, preferred_element_type=jnp.float32).astype(jnp.bfloat16)
    projected = projected.reshape(views, frames * height, row_width, 3 * channels)
    queries = projected[..., :channels].reshape(-1, row_width, channels)
    partner = projected[::-1, :, :, channels:].reshape(-1, row_width, 2 * channels)

    def cross_row(pieces):
        return row_attend(pieces[0], pieces[1][:, :channels], pieces[1][:, channels:])
    cross_mix = lax.map(cross_row, (queries, partner)).reshape(-1, channels)
    stream_b = (tokens_flat.astype(jnp.float32) + jnp.dot(cross_mix, cross_out, preferred_element_type=jnp.float32)).astype(jnp.bfloat16)
    normed_b = layer_norm(stream_b, norm_gains[1])
    projected_t = jnp.dot(normed_b, time_qkv, preferred_element_type=jnp.float32).astype(jnp.bfloat16)
    projected_t = projected_t.reshape(views, frames, height, row_width, 3 * channels)
    regrouped = projected_t.transpose(0, 2, 1, 3, 4).reshape(views * height, frames, row_width, 3 * channels)

    def time_block(pixel_block):
        return time_attend(pixel_block[..., :channels], pixel_block[..., channels:2 * channels], pixel_block[..., 2 * channels:])
    time_mix = lax.map(time_block, regrouped).reshape(views, height, frames, row_width, channels)
    time_mix = time_mix.transpose(0, 2, 1, 3, 4).reshape(-1, channels)
    stream_c = (stream_b.astype(jnp.float32) + jnp.dot(time_mix, time_out, preferred_element_type=jnp.float32)).astype(jnp.bfloat16)
    normed_c = layer_norm(stream_c, norm_gains[2])
    inner_act = jax.nn.gelu(jnp.dot(normed_c, mlp_in, preferred_element_type=jnp.float32), approximate=True).astype(jnp.bfloat16)
    result = (stream_c.astype(jnp.float32) + jnp.dot(inner_act, mlp_out, preferred_element_type=jnp.float32)).astype(jnp.bfloat16)
    return result.reshape(feats.shape)
```

```python
import functools

import jax
import jax.numpy as jnp
import numpy as np
from jax import lax
from jax.experimental import pallas as pl
from jax.experimental.pallas import tpu as pltpu
from jax.sharding import PartitionSpec as P


HEADS = 8


EPSILON = 1e-05


def swapped(value, axis, bit):
    return lax.ppermute(value, axis, [(i, i ^ 1 << bit) for i in range(lax.axis_size(axis))])


def layer_norm(values, norm_gain):
    wide = values.astype(jnp.float32)
    centre = jnp.mean(wide, axis=-1, keepdims=True)
    spread = jnp.mean((wide - centre) ** 2, axis=-1, keepdims=True)
    return ((wide - centre) * lax.rsqrt(spread + EPSILON) * norm_gain).astype(jnp.bfloat16)


def row_attend(queries, key_rows, value_rows):
    length, channels = queries.shape
    head_dim = channels // HEADS
    q_heads = queries.reshape(length, HEADS, head_dim)
    k_heads = key_rows.reshape(length, HEADS, head_dim)
    v_heads = value_rows.reshape(length, HEADS, head_dim)
    scores = jnp.einsum(
        "qhd,khd->hqk", q_heads, k_heads, preferred_element_type=jnp.float32
    ) * head_dim ** (-0.5)
    top_score = jnp.max(scores, axis=-1, keepdims=True)
    expo = jnp.exp(scores - top_score)
    shares = (expo / jnp.sum(expo, axis=-1, keepdims=True)).astype(jnp.bfloat16)
    mixed = jnp.einsum("hqk,khd->qhd", shares, v_heads, preferred_element_type=jnp.float32)
    return mixed.reshape(length, channels).astype(jnp.bfloat16)


def time_attend(queries, key_rows, value_rows):
    frames, pixels, channels = queries.shape
    head_dim = channels // HEADS
    q_heads = queries.reshape(frames, pixels, HEADS, head_dim)
    k_heads = key_rows.reshape(frames, pixels, HEADS, head_dim)
    v_heads = value_rows.reshape(frames, pixels, HEADS, head_dim)
    scores = jnp.einsum(
        "fnhd,gnhd->hfgn", q_heads, k_heads, preferred_element_type=jnp.float32
    ) * head_dim ** (-0.5)
    top_score = jnp.max(scores, axis=2, keepdims=True)
    expo = jnp.exp(scores - top_score)
    shares = (expo / jnp.sum(expo, axis=2, keepdims=True)).astype(jnp.bfloat16)
    mixed = jnp.einsum("hfgn,gnhd->fnhd", shares, v_heads, preferred_element_type=jnp.float32)
    return mixed.reshape(frames, pixels, channels).astype(jnp.bfloat16)


def local_pixels(feats, norm_gains, cross_qkv, cross_out, time_qkv, time_out, mlp_in, mlp_out):
    rows_here, row_width, channels = (feats.shape[2], feats.shape[3], feats.shape[4])
    frame_count = lax.axis_size("frame")
    tokens_flat = feats[0, 0].reshape(-1, channels)
    pixel_count = tokens_flat.shape[0]
    block_pixels = pixel_count // frame_count
    normed_a = layer_norm(tokens_flat, norm_gains[0])
    projected = jnp.dot(normed_a, cross_qkv, preferred_element_type=jnp.float32).astype(
        jnp.bfloat16
    )
    queries = projected[:, :channels]
    partner = swapped(projected[:, channels:], "view", 0)

    def cross_row(pieces):
        return row_attend(pieces[0], pieces[1][:, :channels], pieces[1][:, channels:])

    cross_mix = lax.map(
        cross_row,
        (
            queries.reshape(rows_here, row_width, channels),
            partner.reshape(rows_here, row_width, 2 * channels),
        ),
    )
    cross_mix = cross_mix.reshape(-1, channels)
    stream_b = (
        tokens_flat.astype(jnp.float32)
        + jnp.dot(cross_mix, cross_out, preferred_element_type=jnp.float32)
    ).astype(jnp.bfloat16)
    normed_b = layer_norm(stream_b, norm_gains[1])
    outgoing = normed_b.reshape(1, frame_count, block_pixels, channels)
    gathered = lax.all_to_all(outgoing, "frame", split_axis=1, concat_axis=0, tiled=True)[:, 0]
    frames, pixels, _ = gathered.shape
    projected_b = jnp.dot(
        gathered.reshape(-1, channels), time_qkv, preferred_element_type=jnp.float32
    ).astype(jnp.bfloat16)
    projected_b = projected_b.reshape(frames, pixels, 3 * channels)
    mixed = time_attend(
        projected_b[..., :channels],
        projected_b[..., channels : 2 * channels],
        projected_b[..., 2 * channels :],
    )
    time_mix = mixed[:, None]
    returned = lax.all_to_all(time_mix, "frame", split_axis=0, concat_axis=1, tiled=True).reshape(
        pixel_count, channels
    )
    stream_c = (
        stream_b.astype(jnp.float32)
        + jnp.dot(returned, time_out, preferred_element_type=jnp.float32)
    ).astype(jnp.bfloat16)
    normed_c = layer_norm(stream_c, norm_gains[2])
    inner_act = jax.nn.gelu(
        jnp.dot(normed_c, mlp_in, preferred_element_type=jnp.float32), approximate=True
    ).astype(jnp.bfloat16)
    result = (
        stream_c.astype(jnp.float32)
        + jnp.dot(inner_act, mlp_out, preferred_element_type=jnp.float32)
    ).astype(jnp.bfloat16)
    return result.reshape(1, 1, rows_here, row_width, channels)


LOG2E = 1.4426950408889634


def dot(a, b):
    return jnp.dot(a, b, preferred_element_type=jnp.float32)


def dot_dims(a, b, left, right):
    return lax.dot_general(
        a, b, (((left,), (right,)), ((), ())), preferred_element_type=jnp.float32
    )


def row_kernel(own_ref, other_ref, gains_ref, qkv_ref, out_ref, time_ref, stream_ref, proj_ref, mix_ref):
    channels = own_ref.shape[1]
    length = own_ref.shape[0]
    head_dim = channels // HEADS
    normed = layer_norm(own_ref[...], gains_ref[0:1, :])
    queries = (dot(normed, qkv_ref[:, :channels]) * (head_dim**-0.5 * LOG2E)).astype(jnp.bfloat16)
    other = layer_norm(other_ref[...], gains_ref[0:1, :])
    keys = dot(other, qkv_ref[:, channels : 2 * channels]).astype(jnp.bfloat16)
    values = dot(other, qkv_ref[:, 2 * channels :]).T.astype(jnp.bfloat16)
    lane = lax.broadcasted_iota(jnp.int32, (1, 128), 1)
    ones = jnp.ones((16, length), jnp.bfloat16)
    for head in range(HEADS):
        tile = head * head_dim // 128
        low = head * head_dim - tile * 128
        held = (lane >= low) & (lane < low + head_dim)
        columns = slice(tile * 128, (tile + 1) * 128)
        here = slice(head * head_dim, (head + 1) * head_dim)
        key_part = jnp.where(held, keys[:, columns], jnp.zeros((), jnp.bfloat16))
        scores = dot_dims(key_part, queries[:, columns], 1, 1)
        expo = jnp.exp2(scores - jnp.max(scores, axis=0, keepdims=True)).astype(jnp.bfloat16)
        mixed = dot(jnp.concatenate([values[here, :], ones], axis=0), expo)
        mix_ref[here, :] = (mixed[:head_dim] / mixed[head_dim : head_dim + 1]).astype(jnp.bfloat16)
    stream = own_ref[...].astype(jnp.float32) + dot_dims(mix_ref[...], out_ref[...], 0, 0)
    stream = stream.astype(jnp.bfloat16)
    stream_ref[...] = stream
    normed_b = layer_norm(stream, gains_ref[1:2, :])
    proj_ref[...] = dot(normed_b, time_ref[...]).astype(jnp.bfloat16)


def time_kernel(frames, *refs):
    projs, streams = refs[:frames], refs[frames : 2 * frames]
    gather_ref, spread_ref, out_ref = refs[2 * frames : 2 * frames + 3]
    results = refs[2 * frames + 3 :]
    channels = streams[0].shape[1]
    head_dim = channels // HEADS
    lanes = frames * HEADS
    scores = None
    for f in range(frames):
        query = projs[f][:, :channels].astype(jnp.float32)
        for g in range(frames):
            product = query * projs[g][:, channels : 2 * channels].astype(jnp.float32)
            high = product.astype(jnp.bfloat16)
            low = (product - high.astype(jnp.float32)).astype(jnp.bfloat16)
            part = dot(high, gather_ref[f * frames + g]) + dot(low, gather_ref[f * frames + g])
            scores = part if scores is None else scores + part
    scores = scores * (head_dim**-0.5 * LOG2E)

    def over_frames(op, value):
        step = 1
        while step < frames:
            value = op(value, pltpu.roll(value, step * lanes, 1))
            step *= 2
        return value

    expo = jnp.exp2(scores - over_frames(jnp.maximum, scores))
    shares = (expo / over_frames(jnp.add, expo)).astype(jnp.bfloat16)
    for f in range(frames):
        mixed = None
        for g in range(frames):
            part = dot(shares, spread_ref[f * frames + g]) * projs[g][:, 2 * channels :].astype(
                jnp.float32
            )
            mixed = part if mixed is None else mixed + part
        stream = streams[f][...].astype(jnp.float32) + dot(
            mixed.astype(jnp.bfloat16), out_ref[...]
        )
        results[f][...] = stream.astype(jnp.bfloat16)


def mlp_kernel(stream_ref, gains_ref, in_ref, out_ref, result_ref):
    stream = stream_ref[...]
    normed = layer_norm(stream, gains_ref[2:3, :])
    inner = jax.nn.gelu(dot(normed, in_ref[...]), approximate=True).astype(jnp.bfloat16)
    result_ref[...] = (stream.astype(jnp.float32) + dot(inner, out_ref[...])).astype(jnp.bfloat16)


PARAMS = pltpu.CompilerParams(vmem_limit_bytes=20 * 1024 * 1024)


def attend_row(own, other, norm_gains, cross_qkv, cross_out, time_qkv):
    length, channels = own.shape
    return pl.pallas_call(
        row_kernel,
        out_shape=(
            jax.ShapeDtypeStruct((length, channels), jnp.bfloat16),
            jax.ShapeDtypeStruct((length, 3 * channels), jnp.bfloat16),
        ),
        scratch_shapes=[pltpu.VMEM((channels, length), jnp.bfloat16)],
        compiler_params=PARAMS,
        cost_estimate=pl.CostEstimate(
            flops=2 * length * channels * 7 * channels + 4 * length * length * channels * HEADS,
            bytes_accessed=2 * (6 * length * channels + 7 * channels * channels),
            transcendentals=HEADS * length * length,
        ),
        name="attend_row",
    )(own, other, norm_gains, cross_qkv, cross_out, time_qkv)


def attend_time(projs, streams, time_out):
    frames = len(projs)
    length, channels = streams[0].shape
    head_dim = channels // HEADS
    lanes = frames * frames * HEADS
    gather = np.zeros((frames * frames, channels, lanes), np.float32)
    for f in range(frames):
        for g in range(frames):
            for c in range(channels):
                gather[f * frames + g, c, (g * frames + f) * HEADS + c // head_dim] = 1
    spread = np.swapaxes(gather, 1, 2)
    tile = length // 2
    once = lambda shape: pl.BlockSpec(shape, lambda i: (0,) * len(shape))
    return pl.pallas_call(
        functools.partial(time_kernel, frames),
        grid=(2,),
        in_specs=[pl.BlockSpec((tile, 3 * channels), lambda i: (i, 0))] * frames
        + [pl.BlockSpec((tile, channels), lambda i: (i, 0))] * frames
        + [once(gather.shape), once(spread.shape), once(time_out.shape)],
        out_specs=[pl.BlockSpec((tile, channels), lambda i: (i, 0))] * frames,
        out_shape=[jax.ShapeDtypeStruct((length, channels), jnp.bfloat16)] * frames,
        compiler_params=PARAMS,
        cost_estimate=pl.CostEstimate(
            flops=2 * frames * length * channels * channels,
            bytes_accessed=2 * 5 * frames * length * channels,
            transcendentals=frames * frames * length * HEADS,
        ),
        name="attend_time",
    )(*projs, *streams, jnp.asarray(gather, jnp.bfloat16), jnp.asarray(spread, jnp.bfloat16), time_out)


def mlp_row(stream, norm_gains, mlp_in, mlp_out):
    length, channels = stream.shape
    hidden = mlp_in.shape[1]
    return pl.pallas_call(
        mlp_kernel,
        out_shape=jax.ShapeDtypeStruct((length, channels), jnp.bfloat16),
        compiler_params=PARAMS,
        cost_estimate=pl.CostEstimate(
            flops=4 * length * channels * hidden,
            bytes_accessed=4 * (length * channels + channels * hidden),
            transcendentals=length * hidden,
        ),
        name="mlp_row",
    )(stream, norm_gains, mlp_in, mlp_out)


def frame_swapped(value, distance):
    count = lax.axis_size("frame")
    return lax.ppermute(value, "frame", [(i, i ^ distance) for i in range(count)])


def local_rows(feats, norm_gains, cross_qkv, cross_out, time_qkv, time_out, mlp_in, mlp_out):
    rows_here, _, _ = feats.shape[2:]
    here = lax.axis_index("frame")
    rows = feats[0, 0]
    order = sorted(range(1, rows_here), key=lambda d: (d != 1, d))
    own_rows = {0: lax.dynamic_index_in_dim(rows, here, 0, keepdims=False)}
    for d in order:
        piece = lax.dynamic_index_in_dim(rows, here ^ d, 0, keepdims=False)
        own_rows[d] = frame_swapped(piece, d)
    streams, projs = {}, {}
    for d in [0] + order:
        own = own_rows[d]
        if d:
            own, streams[last] = lax.optimization_barrier((own, streams[last]))
        other = swapped(own, "view", 0)
        streams[d], projs[d] = attend_row(own, other, norm_gains, cross_qkv, cross_out, time_qkv)
        last = d
    frames = list(range(rows_here))
    mixed = attend_time([projs[d] for d in frames], [streams[d] for d in frames], time_out)
    result = jnp.zeros(rows.shape, jnp.bfloat16)
    arrived = []
    for d in order[1:] + order[:1]:
        done = mlp_row(mixed[d], norm_gains, mlp_in, mlp_out)
        arrived.append((here ^ d, frame_swapped(done, d)))
    result = lax.dynamic_update_index_in_dim(
        result, mlp_row(mixed[0], norm_gains, mlp_in, mlp_out), here, 0
    )
    for row, value in arrived:
        result = lax.dynamic_update_index_in_dim(result, value, row, 0)
    return result[None, None]


def local(feats, *rest):
    rows_here = feats.shape[2]
    whole = rows_here == lax.axis_size("frame") and rows_here & (rows_here - 1) == 0
    return (local_rows if whole else local_pixels)(feats, *rest)


def solution(mesh):
    placed = (P(("clips", "view"), "frame", "rows", None, None), P(), P(), P(), P(), P(), P(), P())
    return jax.shard_map(
        local,
        mesh=mesh,
        in_specs=placed,
        out_specs=P(("clips", "view"), "frame", "rows", None, None),
        check_vma=False,
    )
```

```python
import functools

import jax
import jax.numpy as jnp
from jax import lax
from jax.experimental import pallas as pl
from jax.experimental.pallas import tpu as pltpu
from jax.sharding import PartitionSpec as P


HEADS = 8


EPSILON = 1e-05


def swapped(value, axis, bit):
    return lax.ppermute(value, axis, [(i, i ^ 1 << bit) for i in range(lax.axis_size(axis))])


def layer_norm(values, norm_gain):
    wide = values.astype(jnp.float32)
    centre = jnp.mean(wide, axis=-1, keepdims=True)
    spread = jnp.mean((wide - centre) ** 2, axis=-1, keepdims=True)
    return ((wide - centre) * lax.rsqrt(spread + EPSILON) * norm_gain).astype(jnp.bfloat16)


def row_attend(queries, key_rows, value_rows):
    length, channels = queries.shape
    head_dim = channels // HEADS
    q_heads = queries.reshape(length, HEADS, head_dim)
    k_heads = key_rows.reshape(length, HEADS, head_dim)
    v_heads = value_rows.reshape(length, HEADS, head_dim)
    scores = jnp.einsum(
        "qhd,khd->hqk", q_heads, k_heads, preferred_element_type=jnp.float32
    ) * head_dim ** (-0.5)
    top_score = jnp.max(scores, axis=-1, keepdims=True)
    expo = jnp.exp(scores - top_score)
    shares = (expo / jnp.sum(expo, axis=-1, keepdims=True)).astype(jnp.bfloat16)
    mixed = jnp.einsum("hqk,khd->qhd", shares, v_heads, preferred_element_type=jnp.float32)
    return mixed.reshape(length, channels).astype(jnp.bfloat16)


def time_attend(queries, key_rows, value_rows):
    frames, pixels, channels = queries.shape
    head_dim = channels // HEADS
    q_heads = queries.reshape(frames, pixels, HEADS, head_dim)
    k_heads = key_rows.reshape(frames, pixels, HEADS, head_dim)
    v_heads = value_rows.reshape(frames, pixels, HEADS, head_dim)
    scores = jnp.einsum(
        "fnhd,gnhd->hfgn", q_heads, k_heads, preferred_element_type=jnp.float32
    ) * head_dim ** (-0.5)
    top_score = jnp.max(scores, axis=2, keepdims=True)
    expo = jnp.exp(scores - top_score)
    shares = (expo / jnp.sum(expo, axis=2, keepdims=True)).astype(jnp.bfloat16)
    mixed = jnp.einsum("hfgn,gnhd->fnhd", shares, v_heads, preferred_element_type=jnp.float32)
    return mixed.reshape(frames, pixels, channels).astype(jnp.bfloat16)


def local_pixels(feats, norm_gains, cross_qkv, cross_out, time_qkv, time_out, mlp_in, mlp_out):
    rows_here, row_width, channels = (feats.shape[2], feats.shape[3], feats.shape[4])
    frame_count = lax.axis_size("frame")
    tokens_flat = feats[0, 0].reshape(-1, channels)
    pixel_count = tokens_flat.shape[0]
    block_pixels = pixel_count // frame_count
    normed_a = layer_norm(tokens_flat, norm_gains[0])
    projected = jnp.dot(normed_a, cross_qkv, preferred_element_type=jnp.float32).astype(
        jnp.bfloat16
    )
    queries = projected[:, :channels]
    partner = swapped(projected[:, channels:], "view", 0)

    def cross_row(pieces):
        return row_attend(pieces[0], pieces[1][:, :channels], pieces[1][:, channels:])

    cross_mix = lax.map(
        cross_row,
        (
            queries.reshape(rows_here, row_width, channels),
            partner.reshape(rows_here, row_width, 2 * channels),
        ),
    )
    cross_mix = cross_mix.reshape(-1, channels)
    stream_b = (
        tokens_flat.astype(jnp.float32)
        + jnp.dot(cross_mix, cross_out, preferred_element_type=jnp.float32)
    ).astype(jnp.bfloat16)
    normed_b = layer_norm(stream_b, norm_gains[1])
    outgoing = normed_b.reshape(1, frame_count, block_pixels, channels)
    gathered = lax.all_to_all(outgoing, "frame", split_axis=1, concat_axis=0, tiled=True)[:, 0]
    frames, pixels, _ = gathered.shape
    projected_b = jnp.dot(
        gathered.reshape(-1, channels), time_qkv, preferred_element_type=jnp.float32
    ).astype(jnp.bfloat16)
    projected_b = projected_b.reshape(frames, pixels, 3 * channels)
    mixed = time_attend(
        projected_b[..., :channels],
        projected_b[..., channels : 2 * channels],
        projected_b[..., 2 * channels :],
    )
    time_mix = mixed[:, None]
    returned = lax.all_to_all(time_mix, "frame", split_axis=0, concat_axis=1, tiled=True).reshape(
        pixel_count, channels
    )
    stream_c = (
        stream_b.astype(jnp.float32)
        + jnp.dot(returned, time_out, preferred_element_type=jnp.float32)
    ).astype(jnp.bfloat16)
    normed_c = layer_norm(stream_c, norm_gains[2])
    inner_act = jax.nn.gelu(
        jnp.dot(normed_c, mlp_in, preferred_element_type=jnp.float32), approximate=True
    ).astype(jnp.bfloat16)
    result = (
        stream_c.astype(jnp.float32)
        + jnp.dot(inner_act, mlp_out, preferred_element_type=jnp.float32)
    ).astype(jnp.bfloat16)
    return result.reshape(1, 1, rows_here, row_width, channels)


LOG2E = 1.4426950408889634
LANES = 128
PARAMS = pltpu.CompilerParams(vmem_limit_bytes=20 * 1024 * 1024)


def dot(a, b):
    return jnp.dot(a, b, preferred_element_type=jnp.float32)


def dot_dims(a, b, left, right):
    return lax.dot_general(
        a, b, (((left,), (right,)), ((), ())), preferred_element_type=jnp.float32
    )


def row_queries(own_ref, gains_ref, qkv_ref):
    channels = own_ref.shape[1]
    normed = layer_norm(own_ref[...], gains_ref[0:1, :])
    return dot(normed, qkv_ref[:, :channels]).astype(jnp.bfloat16)


def row_keys_values(other_ref, gains_ref, qkv_ref):
    channels = other_ref.shape[1]
    normed = layer_norm(other_ref[...], gains_ref[0:1, :])
    keys = dot(normed, qkv_ref[:, channels : 2 * channels]).astype(jnp.bfloat16)
    values = dot(normed, qkv_ref[:, 2 * channels :]).astype(jnp.bfloat16)
    return keys, values.T


def cross_heads(queries, keys, values, mix_ref):
    length, channels = keys.shape
    head_dim = channels // HEADS
    lane = lax.broadcasted_iota(jnp.int32, (1, LANES), 1)
    ones = jnp.ones((16, length), jnp.bfloat16)
    for head in range(HEADS):
        tile = head * head_dim // LANES
        low = head * head_dim - tile * LANES
        held = (lane >= low) & (lane < low + head_dim)
        columns = slice(tile * LANES, (tile + 1) * LANES)
        here = slice(head * head_dim, (head + 1) * head_dim)
        key_part = jnp.where(held, keys[:, columns], jnp.zeros((), jnp.bfloat16))
        scores = dot_dims(key_part, queries[:, columns], 1, 1)
        top = jnp.max(scores, axis=0, keepdims=True)
        expo = jnp.exp2((scores - top) * (head_dim**-0.5 * LOG2E)).astype(jnp.bfloat16)
        mixed = dot(jnp.concatenate([values[here, :], ones], axis=0), expo)
        mix_ref[here, :] = (mixed[:head_dim] / mixed[head_dim : head_dim + 1]).astype(jnp.bfloat16)


def after_cross(own, mix_ref, gains_ref, out_ref, time_ref):
    stream = own.astype(jnp.float32) + dot_dims(mix_ref[...], out_ref[...], 0, 0)
    stream = stream.astype(jnp.bfloat16)
    normed = layer_norm(stream, gains_ref[1:2, :])
    return stream, dot_dims(time_ref[...], normed, 0, 1).astype(jnp.bfloat16)


def row_kernel(own_ref, other_ref, gains_ref, qkv_ref, out_ref, time_ref, stream_ref, proj_ref, mix_ref):
    queries = row_queries(own_ref, gains_ref, qkv_ref)
    keys, values = row_keys_values(other_ref, gains_ref, qkv_ref)
    cross_heads(queries, keys, values, mix_ref)
    stream_ref[...], proj_ref[...] = after_cross(
        own_ref[...], mix_ref, gains_ref, out_ref, time_ref
    )


def time_heads(projs, pixels, mixes):
    frames = len(projs)
    channels = mixes[0].shape[0]
    head_dim = channels // HEADS

    def one_head(head, _):
        def rows(ref, part):
            start = pl.multiple_of(part * channels + head * head_dim, head_dim)
            return ref[pl.ds(start, head_dim), pixels].astype(jnp.float32)

        keys = [rows(ref, 1) for ref in projs]
        values = [rows(ref, 2) for ref in projs]
        for f in range(frames):
            query = rows(projs[f], 0)
            scores = [jnp.sum(query * key, axis=0, keepdims=True) for key in keys]
            top = functools.reduce(jnp.maximum, scores)
            expo = [jnp.exp2((s - top) * (head_dim**-0.5 * LOG2E)) for s in scores]
            over = 1.0 / functools.reduce(jnp.add, expo)
            mixed = None
            for g in range(frames):
                share = (expo[g] * over).astype(jnp.bfloat16).astype(jnp.float32)
                part = share * values[g]
                mixed = part if mixed is None else mixed + part
            start = pl.multiple_of(head * head_dim, head_dim)
            mixes[f][pl.ds(start, head_dim), :] = mixed.astype(jnp.bfloat16)
        return 0

    lax.fori_loop(0, HEADS, one_head, 0)


def finish_tail(
    own, mix_ref, first, gains_ref, out_ref, time_ref, time_out_ref, projs, streams, proj_ref, mixes, results
):
    count = own.shape[0]
    stream, proj_ref[...] = after_cross(own, mix_ref, gains_ref, out_ref, time_ref)
    time_heads(
        [ref.at[:, first : first + count] for ref in projs] + [proj_ref], slice(None), mixes
    )
    before = [ref[first : first + count, :] for ref in streams] + [stream]
    for f, result in enumerate(results):
        result[...] = (
            before[f].astype(jnp.float32) + dot_dims(mixes[f][...], time_out_ref[...], 0, 0)
        ).astype(jnp.bfloat16)


def finish_head_kernel(frames, own_ref, other_ref, gains_ref, qkv_ref, out_ref, time_ref, time_out_ref, *refs):
    projs, streams = refs[: frames - 1], refs[frames - 1 : 2 * frames - 2]
    refs = refs[2 * frames - 2 :]
    results, refs = refs[:frames], refs[frames:]
    queries_ref, keys_ref, values_ref, mix_ref, proj_ref = refs[:5]
    count = results[0].shape[0]
    queries = row_queries(own_ref, gains_ref, qkv_ref)
    keys, values = row_keys_values(other_ref, gains_ref, qkv_ref)
    queries_ref[...] = queries[count:]
    keys_ref[...] = keys
    values_ref[...] = values
    cross_heads(queries[:count], keys, values, mix_ref)
    finish_tail(
        own_ref[:count, :], mix_ref, 0, gains_ref, out_ref, time_ref, time_out_ref,
        projs, streams, proj_ref, refs[5:], results,
    )


def finish_rest_kernel(
    frames, own_ref, queries_ref, keys_ref, values_ref, gains_ref, out_ref, time_ref, time_out_ref, *refs
):
    projs, streams = refs[: frames - 1], refs[frames - 1 : 2 * frames - 2]
    refs = refs[2 * frames - 2 :]
    results, refs = refs[:frames], refs[frames:]
    count = results[0].shape[0]
    first = own_ref.shape[0] - count
    cross_heads(queries_ref[...], keys_ref[...], values_ref[...], refs[0])
    finish_tail(
        own_ref[first:, :], refs[0], first, gains_ref, out_ref, time_ref, time_out_ref,
        projs, streams, refs[1], refs[2:], results,
    )


def mlp_kernel(pieces, *refs):
    gains_ref, in_ref, out_ref, result_ref = refs[pieces:]
    first = 0
    for ref in refs[:pieces]:
        stream = ref[...]
        normed = layer_norm(stream, gains_ref[2:3, :])
        inner = jax.nn.gelu(dot(normed, in_ref[...]), approximate=True).astype(jnp.bfloat16)
        result_ref[first : first + stream.shape[0], :] = (
            stream.astype(jnp.float32) + dot(inner, out_ref[...])
        ).astype(jnp.bfloat16)
        first += stream.shape[0]


def array(*shape):
    return jax.ShapeDtypeStruct(shape, jnp.bfloat16)


def attend_row(own, other, norm_gains, cross_qkv, cross_out, time_qkv):
    length, channels = own.shape
    return pl.pallas_call(
        row_kernel,
        out_shape=(array(length, channels), array(3 * channels, length)),
        scratch_shapes=[pltpu.VMEM((channels, length), jnp.bfloat16)],
        compiler_params=PARAMS,
        cost_estimate=pl.CostEstimate(
            flops=2 * length * channels * 7 * channels + 4 * length * length * channels * HEADS,
            bytes_accessed=2 * (6 * length * channels + 7 * channels * channels),
            transcendentals=HEADS * length * length,
        ),
        name="attend_row",
    )(own, other, norm_gains, cross_qkv, cross_out, time_qkv)


def finish_cost(length, count, channels, frames):
    return pl.CostEstimate(
        flops=2 * length * channels * 3 * channels + 4 * length * count * channels * HEADS,
        bytes_accessed=2 * (8 * frames * count * channels + 8 * channels * channels),
        transcendentals=HEADS * length * count,
    )


def finish_scratch(count, channels, frames):
    return (
        [pltpu.VMEM((channels, count), jnp.bfloat16)]
        + [pltpu.VMEM((3 * channels, count), jnp.bfloat16)]
        + [pltpu.VMEM((channels, count), jnp.bfloat16)] * frames
    )


def finish_head(count, own, other, weights, time_out, projs, streams):
    norm_gains, cross_qkv, cross_out, time_qkv = weights
    length, channels = own.shape
    frames = len(projs) + 1
    out = pl.pallas_call(
        functools.partial(finish_head_kernel, frames),
        out_shape=[array(count, channels)] * frames
        + [array(length - count, channels), array(length, channels), array(channels, length)],
        scratch_shapes=finish_scratch(count, channels, frames),
        compiler_params=PARAMS,
        cost_estimate=finish_cost(length, count, channels, frames),
        name="finish_head",
    )(own, other, norm_gains, cross_qkv, cross_out, time_qkv, time_out, *projs, *streams)
    return out[:frames], out[frames:]


def finish_rest(own, kept, weights, time_out, projs, streams):
    norm_gains, _, cross_out, time_qkv = weights
    length, channels = own.shape
    frames = len(projs) + 1
    count = kept[0].shape[0]
    return pl.pallas_call(
        functools.partial(finish_rest_kernel, frames),
        out_shape=[array(count, channels)] * frames,
        scratch_shapes=finish_scratch(count, channels, frames),
        compiler_params=PARAMS,
        cost_estimate=finish_cost(length, count, channels, frames),
        name="finish_rest",
    )(own, *kept, norm_gains, cross_out, time_qkv, time_out, *projs, *streams)


def mlp(pieces, norm_gains, mlp_in, mlp_out):
    channels, hidden = mlp_in.shape
    length = sum(piece.shape[0] for piece in pieces)
    return pl.pallas_call(
        functools.partial(mlp_kernel, len(pieces)),
        out_shape=array(length, channels),
        compiler_params=PARAMS,
        cost_estimate=pl.CostEstimate(
            flops=4 * length * channels * hidden,
            bytes_accessed=4 * (length * channels + channels * hidden),
            transcendentals=length * hidden,
        ),
        name="mlp",
    )(*pieces, norm_gains, mlp_in, mlp_out)


def frame_swapped(value, distance):
    count = lax.axis_size("frame")
    return lax.ppermute(value, "frame", [(i, i ^ distance) for i in range(count)])


def local_rows(feats, norm_gains, cross_qkv, cross_out, time_qkv, time_out, mlp_in, mlp_out):
    rows_here, row_width, _ = feats.shape[2:]
    here = lax.axis_index("frame")
    rows = feats[0, 0]
    weights = (norm_gains, cross_qkv, cross_out, time_qkv)
    order = list(range(1, rows_here))
    own_rows = {0: lax.dynamic_index_in_dim(rows, here, 0, keepdims=False)}
    for d in order:
        piece = lax.dynamic_index_in_dim(rows, here ^ d, 0, keepdims=False)
        own_rows[d] = frame_swapped(piece, d)
    streams, projs = [], []
    for d in [0] + order:
        own = own_rows[d]
        if d:
            own, streams[-1] = lax.optimization_barrier((own, streams[-1]))
        other = swapped(own, "view", 0)
        if d == order[-1]:
            break
        stream, proj = attend_row(own, other, *weights)
        streams.append(stream)
        projs.append(proj)
    count = min(row_width, 2 * LANES)
    early, kept = finish_head(count, own, other, weights, time_out, projs, streams)
    late = finish_rest(own, kept, weights, time_out, projs, streams)
    far = order[1:]
    result = jnp.zeros(rows.shape, jnp.bfloat16)
    arrived = []
    for pieces, first in ((early, 0), (late, count)):
        for d in far:
            done = mlp([pieces[d]], norm_gains, mlp_in, mlp_out)
            arrived.append((here ^ d, first, frame_swapped(done, d)))
    near = mlp([early[1], late[1]], norm_gains, mlp_in, mlp_out)
    arrived.append((here ^ 1, 0, frame_swapped(near, 1)))
    own_result = mlp([early[0], late[0]], norm_gains, mlp_in, mlp_out)
    arrived.insert(0, (here, 0, own_result))
    for row, first, value in arrived:
        result = lax.dynamic_update_slice(result, value[None], (row, first, 0))
    return result[None, None]


def local(feats, *rest):
    rows_here = feats.shape[2]
    whole = rows_here == lax.axis_size("frame") and rows_here & (rows_here - 1) == 0
    return (local_rows if whole else local_pixels)(feats, *rest)


def solution(mesh):
    placed = (P(("clips", "view"), "frame", "rows", None, None), P(), P(), P(), P(), P(), P(), P())
    return jax.shard_map(
        local,
        mesh=mesh,
        in_specs=placed,
        out_specs=P(("clips", "view"), "frame", "rows", None, None),
        check_vma=False,
    )
```

```python
import functools

import jax
import jax.numpy as jnp
from jax import lax
from jax.experimental import pallas as pl
from jax.experimental.pallas import tpu as pltpu
from jax.sharding import PartitionSpec as P


HEADS = 8


EPSILON = 1e-05


def swapped(value, axis, bit):
    return lax.ppermute(value, axis, [(i, i ^ 1 << bit) for i in range(lax.axis_size(axis))])


def layer_norm(values, norm_gain):
    wide = values.astype(jnp.float32)
    centre = jnp.mean(wide, axis=-1, keepdims=True)
    spread = jnp.mean((wide - centre) ** 2, axis=-1, keepdims=True)
    return ((wide - centre) * lax.rsqrt(spread + EPSILON) * norm_gain).astype(jnp.bfloat16)


def row_attend(queries, key_rows, value_rows):
    length, channels = queries.shape
    head_dim = channels // HEADS
    q_heads = queries.reshape(length, HEADS, head_dim)
    k_heads = key_rows.reshape(length, HEADS, head_dim)
    v_heads = value_rows.reshape(length, HEADS, head_dim)
    scores = jnp.einsum(
        "qhd,khd->hqk", q_heads, k_heads, preferred_element_type=jnp.float32
    ) * head_dim ** (-0.5)
    top_score = jnp.max(scores, axis=-1, keepdims=True)
    expo = jnp.exp(scores - top_score)
    shares = (expo / jnp.sum(expo, axis=-1, keepdims=True)).astype(jnp.bfloat16)
    mixed = jnp.einsum("hqk,khd->qhd", shares, v_heads, preferred_element_type=jnp.float32)
    return mixed.reshape(length, channels).astype(jnp.bfloat16)


def time_attend(queries, key_rows, value_rows):
    frames, pixels, channels = queries.shape
    head_dim = channels // HEADS
    q_heads = queries.reshape(frames, pixels, HEADS, head_dim)
    k_heads = key_rows.reshape(frames, pixels, HEADS, head_dim)
    v_heads = value_rows.reshape(frames, pixels, HEADS, head_dim)
    scores = jnp.einsum(
        "fnhd,gnhd->hfgn", q_heads, k_heads, preferred_element_type=jnp.float32
    ) * head_dim ** (-0.5)
    top_score = jnp.max(scores, axis=2, keepdims=True)
    expo = jnp.exp(scores - top_score)
    shares = (expo / jnp.sum(expo, axis=2, keepdims=True)).astype(jnp.bfloat16)
    mixed = jnp.einsum("hfgn,gnhd->fnhd", shares, v_heads, preferred_element_type=jnp.float32)
    return mixed.reshape(frames, pixels, channels).astype(jnp.bfloat16)


def local_pixels(feats, norm_gains, cross_qkv, cross_out, time_qkv, time_out, mlp_in, mlp_out):
    rows_here, row_width, channels = (feats.shape[2], feats.shape[3], feats.shape[4])
    frame_count = lax.axis_size("frame")
    tokens_flat = feats[0, 0].reshape(-1, channels)
    pixel_count = tokens_flat.shape[0]
    block_pixels = pixel_count // frame_count
    normed_a = layer_norm(tokens_flat, norm_gains[0])
    projected = jnp.dot(normed_a, cross_qkv, preferred_element_type=jnp.float32).astype(
        jnp.bfloat16
    )
    queries = projected[:, :channels]
    partner = swapped(projected[:, channels:], "view", 0)

    def cross_row(pieces):
        return row_attend(pieces[0], pieces[1][:, :channels], pieces[1][:, channels:])

    cross_mix = lax.map(
        cross_row,
        (
            queries.reshape(rows_here, row_width, channels),
            partner.reshape(rows_here, row_width, 2 * channels),
        ),
    )
    cross_mix = cross_mix.reshape(-1, channels)
    stream_b = (
        tokens_flat.astype(jnp.float32)
        + jnp.dot(cross_mix, cross_out, preferred_element_type=jnp.float32)
    ).astype(jnp.bfloat16)
    normed_b = layer_norm(stream_b, norm_gains[1])
    outgoing = normed_b.reshape(1, frame_count, block_pixels, channels)
    gathered = lax.all_to_all(outgoing, "frame", split_axis=1, concat_axis=0, tiled=True)[:, 0]
    frames, pixels, _ = gathered.shape
    projected_b = jnp.dot(
        gathered.reshape(-1, channels), time_qkv, preferred_element_type=jnp.float32
    ).astype(jnp.bfloat16)
    projected_b = projected_b.reshape(frames, pixels, 3 * channels)
    mixed = time_attend(
        projected_b[..., :channels],
        projected_b[..., channels : 2 * channels],
        projected_b[..., 2 * channels :],
    )
    time_mix = mixed[:, None]
    returned = lax.all_to_all(time_mix, "frame", split_axis=0, concat_axis=1, tiled=True).reshape(
        pixel_count, channels
    )
    stream_c = (
        stream_b.astype(jnp.float32)
        + jnp.dot(returned, time_out, preferred_element_type=jnp.float32)
    ).astype(jnp.bfloat16)
    normed_c = layer_norm(stream_c, norm_gains[2])
    inner_act = jax.nn.gelu(
        jnp.dot(normed_c, mlp_in, preferred_element_type=jnp.float32), approximate=True
    ).astype(jnp.bfloat16)
    result = (
        stream_c.astype(jnp.float32)
        + jnp.dot(inner_act, mlp_out, preferred_element_type=jnp.float32)
    ).astype(jnp.bfloat16)
    return result.reshape(1, 1, rows_here, row_width, channels)


LOG2E = 1.4426950408889634
LANES = 128
PARAMS = pltpu.CompilerParams(vmem_limit_bytes=20 * 1024 * 1024)


def dot(a, b):
    return jnp.dot(a, b, preferred_element_type=jnp.float32)


def dot_dims(a, b, left, right):
    return lax.dot_general(
        a, b, (((left,), (right,)), ((), ())), preferred_element_type=jnp.float32
    )


def row_queries(own_ref, gains_ref, qkv_ref):
    channels = own_ref.shape[1]
    normed = layer_norm(own_ref[...], gains_ref[0:1, :])
    return dot(normed, qkv_ref[:, :channels]).astype(jnp.bfloat16)


def row_keys_values(other_ref, gains_ref, qkv_ref):
    channels = other_ref.shape[1]
    normed = layer_norm(other_ref[...], gains_ref[0:1, :])
    keys = dot(normed, qkv_ref[:, channels : 2 * channels]).astype(jnp.bfloat16)
    values = dot(normed, qkv_ref[:, 2 * channels :]).astype(jnp.bfloat16)
    return keys, values.T


def cross_heads(queries, keys, values, mix_ref):
    length, channels = keys.shape
    head_dim = channels // HEADS
    lane = lax.broadcasted_iota(jnp.int32, (1, LANES), 1)
    ones = jnp.ones((16, length), jnp.bfloat16)

    def head_scores(head):
        tile = head * head_dim // LANES
        low = head * head_dim - tile * LANES
        held = (lane >= low) & (lane < low + head_dim)
        columns = slice(tile * LANES, (tile + 1) * LANES)
        key_part = jnp.where(held, keys[:, columns], jnp.zeros((), jnp.bfloat16))
        return dot_dims(key_part, queries[:, columns], 1, 1)

    ahead = head_scores(0)
    for head in range(HEADS):
        scores = ahead
        if head + 1 < HEADS:
            ahead = head_scores(head + 1)
        top = jnp.max(scores, axis=0, keepdims=True)
        expo = jnp.exp2((scores - top) * (head_dim**-0.5 * LOG2E)).astype(jnp.bfloat16)
        here = slice(head * head_dim, (head + 1) * head_dim)
        mixed = dot(jnp.concatenate([values[here, :], ones], axis=0), expo)
        over = 1.0 / mixed[head_dim : head_dim + 1]
        mix_ref[here, :] = (mixed[:head_dim] * over).astype(jnp.bfloat16)


def after_cross(own, mix_ref, gains_ref, out_ref, time_ref):
    stream = own.astype(jnp.float32) + dot_dims(mix_ref[...], out_ref[...], 0, 0)
    stream = stream.astype(jnp.bfloat16)
    normed = layer_norm(stream, gains_ref[1:2, :])
    return stream, dot_dims(time_ref[...], normed, 0, 1).astype(jnp.bfloat16)


def row_kernel(own_ref, other_ref, gains_ref, qkv_ref, out_ref, time_ref, stream_ref, proj_ref, mix_ref):
    queries = row_queries(own_ref, gains_ref, qkv_ref)
    keys, values = row_keys_values(other_ref, gains_ref, qkv_ref)
    cross_heads(queries, keys, values, mix_ref)
    stream_ref[...], proj_ref[...] = after_cross(
        own_ref[...], mix_ref, gains_ref, out_ref, time_ref
    )


def time_heads(projs, pixels, mixes):
    frames = len(projs)
    channels = mixes[0].shape[0]
    head_dim = channels // HEADS

    def one_head(head, _):
        def rows(ref, part):
            start = pl.multiple_of(part * channels + head * head_dim, head_dim)
            return ref[pl.ds(start, head_dim), pixels].astype(jnp.float32)

        keys = [rows(ref, 1) for ref in projs]
        values = [rows(ref, 2) for ref in projs]
        for f in range(frames):
            query = rows(projs[f], 0)
            scores = [jnp.sum(query * key, axis=0, keepdims=True) for key in keys]
            top = functools.reduce(jnp.maximum, scores)
            expo = [jnp.exp2((s - top) * (head_dim**-0.5 * LOG2E)) for s in scores]
            over = 1.0 / functools.reduce(jnp.add, expo)
            mixed = None
            for g in range(frames):
                share = (expo[g] * over).astype(jnp.bfloat16).astype(jnp.float32)
                part = share * values[g]
                mixed = part if mixed is None else mixed + part
            start = pl.multiple_of(head * head_dim, head_dim)
            mixes[f][pl.ds(start, head_dim), :] = mixed.astype(jnp.bfloat16)
        return 0

    lax.fori_loop(0, HEADS, one_head, 0)


def finish_tail(
    own, mix_ref, first, gains_ref, out_ref, time_ref, time_out_ref, projs, streams, proj_ref, mixes, results
):
    count = own.shape[0]
    stream, proj_ref[...] = after_cross(own, mix_ref, gains_ref, out_ref, time_ref)
    time_heads(
        [ref.at[:, first : first + count] for ref in projs] + [proj_ref], slice(None), mixes
    )
    before = [ref[first : first + count, :] for ref in streams] + [stream]
    for f, result in enumerate(results):
        result[...] = (
            before[f].astype(jnp.float32) + dot_dims(mixes[f][...], time_out_ref[...], 0, 0)
        ).astype(jnp.bfloat16)


def finish_head_kernel(frames, own_ref, other_ref, gains_ref, qkv_ref, out_ref, time_ref, time_out_ref, *refs):
    projs, streams = refs[: frames - 1], refs[frames - 1 : 2 * frames - 2]
    refs = refs[2 * frames - 2 :]
    results, refs = refs[:frames], refs[frames:]
    queries_ref, keys_ref, values_ref, mix_ref, proj_ref = refs[:5]
    count = results[0].shape[0]
    queries = row_queries(own_ref, gains_ref, qkv_ref)
    keys, values = row_keys_values(other_ref, gains_ref, qkv_ref)
    queries_ref[...] = queries[count:]
    keys_ref[...] = keys
    values_ref[...] = values
    cross_heads(queries[:count], keys, values, mix_ref)
    finish_tail(
        own_ref[:count, :], mix_ref, 0, gains_ref, out_ref, time_ref, time_out_ref,
        projs, streams, proj_ref, refs[5:], results,
    )


def finish_rest_kernel(
    frames, own_ref, queries_ref, keys_ref, values_ref, gains_ref, out_ref, time_ref, time_out_ref, *refs
):
    projs, streams = refs[: frames - 1], refs[frames - 1 : 2 * frames - 2]
    refs = refs[2 * frames - 2 :]
    results, refs = refs[:frames], refs[frames:]
    count = results[0].shape[0]
    first = own_ref.shape[0] - count
    cross_heads(queries_ref[...], keys_ref[...], values_ref[...], refs[0])
    finish_tail(
        own_ref[first:, :], refs[0], first, gains_ref, out_ref, time_ref, time_out_ref,
        projs, streams, refs[1], refs[2:], results,
    )


def mlp_kernel(pieces, *refs):
    gains_ref, in_ref, out_ref, result_ref = refs[pieces:]
    first = 0
    for ref in refs[:pieces]:
        stream = ref[...]
        normed = layer_norm(stream, gains_ref[2:3, :])
        inner = jax.nn.gelu(dot(normed, in_ref[...]), approximate=True).astype(jnp.bfloat16)
        result_ref[first : first + stream.shape[0], :] = (
            stream.astype(jnp.float32) + dot(inner, out_ref[...])
        ).astype(jnp.bfloat16)
        first += stream.shape[0]


def array(*shape):
    return jax.ShapeDtypeStruct(shape, jnp.bfloat16)


def attend_row(own, other, norm_gains, cross_qkv, cross_out, time_qkv):
    length, channels = own.shape
    return pl.pallas_call(
        row_kernel,
        out_shape=(array(length, channels), array(3 * channels, length)),
        scratch_shapes=[pltpu.VMEM((channels, length), jnp.bfloat16)],
        compiler_params=PARAMS,
        cost_estimate=pl.CostEstimate(
            flops=2 * length * channels * 7 * channels + 4 * length * length * channels * HEADS,
            bytes_accessed=2 * (6 * length * channels + 7 * channels * channels),
            transcendentals=HEADS * length * length,
        ),
        name="attend_row",
    )(own, other, norm_gains, cross_qkv, cross_out, time_qkv)


def finish_cost(length, count, channels, frames):
    return pl.CostEstimate(
        flops=2 * length * channels * 3 * channels + 4 * length * count * channels * HEADS,
        bytes_accessed=2 * (8 * frames * count * channels + 8 * channels * channels),
        transcendentals=HEADS * length * count,
    )


def finish_scratch(count, channels, frames):
    return (
        [pltpu.VMEM((channels, count), jnp.bfloat16)]
        + [pltpu.VMEM((3 * channels, count), jnp.bfloat16)]
        + [pltpu.VMEM((channels, count), jnp.bfloat16)] * frames
    )


def finish_head(count, own, other, weights, time_out, projs, streams):
    norm_gains, cross_qkv, cross_out, time_qkv = weights
    length, channels = own.shape
    frames = len(projs) + 1
    out = pl.pallas_call(
        functools.partial(finish_head_kernel, frames),
        out_shape=[array(count, channels)] * frames
        + [array(length - count, channels), array(length, channels), array(channels, length)],
        scratch_shapes=finish_scratch(count, channels, frames),
        compiler_params=PARAMS,
        cost_estimate=finish_cost(length, count, channels, frames),
        name="finish_head",
    )(own, other, norm_gains, cross_qkv, cross_out, time_qkv, time_out, *projs, *streams)
    return out[:frames], out[frames:]


def finish_rest(own, kept, weights, time_out, projs, streams):
    norm_gains, _, cross_out, time_qkv = weights
    length, channels = own.shape
    frames = len(projs) + 1
    count = kept[0].shape[0]
    return pl.pallas_call(
        functools.partial(finish_rest_kernel, frames),
        out_shape=[array(count, channels)] * frames,
        scratch_shapes=finish_scratch(count, channels, frames),
        compiler_params=PARAMS,
        cost_estimate=finish_cost(length, count, channels, frames),
        name="finish_rest",
    )(own, *kept, norm_gains, cross_out, time_qkv, time_out, *projs, *streams)


def mlp(pieces, norm_gains, mlp_in, mlp_out):
    channels, hidden = mlp_in.shape
    length = sum(piece.shape[0] for piece in pieces)
    return pl.pallas_call(
        functools.partial(mlp_kernel, len(pieces)),
        out_shape=array(length, channels),
        compiler_params=PARAMS,
        cost_estimate=pl.CostEstimate(
            flops=4 * length * channels * hidden,
            bytes_accessed=4 * (length * channels + channels * hidden),
            transcendentals=length * hidden,
        ),
        name="mlp",
    )(*pieces, norm_gains, mlp_in, mlp_out)


def copy_kernel(after_ref, value_ref, result_ref):
    result_ref[...] = value_ref[...]


def copied_after(after, value):
    return pl.pallas_call(
        copy_kernel,
        out_shape=jax.ShapeDtypeStruct(value.shape, value.dtype),
        in_specs=[pl.BlockSpec(memory_space=pl.ANY), pl.BlockSpec(memory_space=pltpu.VMEM)],
        out_specs=pl.BlockSpec(memory_space=pltpu.VMEM),
        compiler_params=PARAMS,
        cost_estimate=pl.CostEstimate(flops=0, bytes_accessed=0, transcendentals=0),
        name="copied_after",
    )(after, value)


def frame_swapped(value, distance):
    count = lax.axis_size("frame")
    return lax.ppermute(value, "frame", [(i, i ^ distance) for i in range(count)])


def local_rows(feats, norm_gains, cross_qkv, cross_out, time_qkv, time_out, mlp_in, mlp_out):
    rows_here, row_width, _ = feats.shape[2:]
    here = lax.axis_index("frame")
    rows = feats[0, 0]
    weights = (norm_gains, cross_qkv, cross_out, time_qkv)
    order = list(range(1, rows_here))
    own_rows = {0: lax.dynamic_index_in_dim(rows, here, 0, keepdims=False)}
    for d in order:
        piece = lax.dynamic_index_in_dim(rows, here ^ d, 0, keepdims=False)
        own_rows[d] = frame_swapped(piece, d)
    streams, projs = [], []
    for d in [0] + order:
        own = own_rows[d]
        if d:
            own, streams[-1] = lax.optimization_barrier((own, streams[-1]))
        other = swapped(own, "view", 0)
        if d == order[-1]:
            break
        stream, proj = attend_row(own, other, *weights)
        if d == 0:
            weights = (copied_after(stream, norm_gains),) + weights[1:]
        streams.append(stream)
        projs.append(proj)
    count = min(row_width, 2 * LANES)
    early, kept = finish_head(count, own, other, weights, time_out, projs, streams)
    late = finish_rest(own, kept, weights, time_out, projs, streams)
    far = order[1:]
    result = jnp.zeros(rows.shape, jnp.bfloat16)
    arrived = []

    def send(pieces, d, first):
        done = mlp(pieces, norm_gains, mlp_in, mlp_out)
        arrived.append((here ^ d, first, frame_swapped(done, d)))

    for d in far:
        send([early[d]], d, 0)
    for d in far:
        send([late[d]], d, count)
    send([early[1], late[1]], 1, 0)
    own_result = mlp([early[0], late[0]], norm_gains, mlp_in, mlp_out)
    arrived.insert(0, (here, 0, own_result))
    for row, first, value in arrived:
        result = lax.dynamic_update_slice(result, value[None], (row, first, 0))
    return result[None, None]


def local(feats, *rest):
    rows_here = feats.shape[2]
    whole = rows_here == lax.axis_size("frame") and rows_here & (rows_here - 1) == 0
    return (local_rows if whole else local_pixels)(feats, *rest)


def solution(mesh):
    placed = (P(("clips", "view"), "frame", "rows", None, None), P(), P(), P(), P(), P(), P(), P())
    return jax.shard_map(
        local,
        mesh=mesh,
        in_specs=placed,
        out_specs=P(("clips", "view"), "frame", "rows", None, None),
        check_vma=False,
    )
```

```python
import functools

import jax
import jax.numpy as jnp
from jax import lax
from jax.experimental import pallas as pl
from jax.experimental.pallas import tpu as pltpu
from jax.sharding import PartitionSpec as P


HEADS = 8


EPSILON = 1e-05


def swapped(value, axis, bit):
    return lax.ppermute(value, axis, [(i, i ^ 1 << bit) for i in range(lax.axis_size(axis))])


def layer_norm(values, norm_gain):
    wide = values.astype(jnp.float32)
    centre = jnp.mean(wide, axis=-1, keepdims=True)
    spread = jnp.mean((wide - centre) ** 2, axis=-1, keepdims=True)
    return ((wide - centre) * lax.rsqrt(spread + EPSILON) * norm_gain).astype(jnp.bfloat16)


def row_attend(queries, key_rows, value_rows):
    length, channels = queries.shape
    head_dim = channels // HEADS
    q_heads = queries.reshape(length, HEADS, head_dim)
    k_heads = key_rows.reshape(length, HEADS, head_dim)
    v_heads = value_rows.reshape(length, HEADS, head_dim)
    scores = jnp.einsum(
        "qhd,khd->hqk", q_heads, k_heads, preferred_element_type=jnp.float32
    ) * head_dim ** (-0.5)
    top_score = jnp.max(scores, axis=-1, keepdims=True)
    expo = jnp.exp(scores - top_score)
    shares = (expo / jnp.sum(expo, axis=-1, keepdims=True)).astype(jnp.bfloat16)
    mixed = jnp.einsum("hqk,khd->qhd", shares, v_heads, preferred_element_type=jnp.float32)
    return mixed.reshape(length, channels).astype(jnp.bfloat16)


def time_attend(queries, key_rows, value_rows):
    frames, pixels, channels = queries.shape
    head_dim = channels // HEADS
    q_heads = queries.reshape(frames, pixels, HEADS, head_dim)
    k_heads = key_rows.reshape(frames, pixels, HEADS, head_dim)
    v_heads = value_rows.reshape(frames, pixels, HEADS, head_dim)
    scores = jnp.einsum(
        "fnhd,gnhd->hfgn", q_heads, k_heads, preferred_element_type=jnp.float32
    ) * head_dim ** (-0.5)
    top_score = jnp.max(scores, axis=2, keepdims=True)
    expo = jnp.exp(scores - top_score)
    shares = (expo / jnp.sum(expo, axis=2, keepdims=True)).astype(jnp.bfloat16)
    mixed = jnp.einsum("hfgn,gnhd->fnhd", shares, v_heads, preferred_element_type=jnp.float32)
    return mixed.reshape(frames, pixels, channels).astype(jnp.bfloat16)


def local_pixels(feats, norm_gains, cross_qkv, cross_out, time_qkv, time_out, mlp_in, mlp_out):
    rows_here, row_width, channels = (feats.shape[2], feats.shape[3], feats.shape[4])
    frame_count = lax.axis_size("frame")
    tokens_flat = feats[0, 0].reshape(-1, channels)
    pixel_count = tokens_flat.shape[0]
    block_pixels = pixel_count // frame_count
    normed_a = layer_norm(tokens_flat, norm_gains[0])
    projected = jnp.dot(normed_a, cross_qkv, preferred_element_type=jnp.float32).astype(
        jnp.bfloat16
    )
    queries = projected[:, :channels]
    partner = swapped(projected[:, channels:], "view", 0)

    def cross_row(pieces):
        return row_attend(pieces[0], pieces[1][:, :channels], pieces[1][:, channels:])

    cross_mix = lax.map(
        cross_row,
        (
            queries.reshape(rows_here, row_width, channels),
            partner.reshape(rows_here, row_width, 2 * channels),
        ),
    )
    cross_mix = cross_mix.reshape(-1, channels)
    stream_b = (
        tokens_flat.astype(jnp.float32)
        + jnp.dot(cross_mix, cross_out, preferred_element_type=jnp.float32)
    ).astype(jnp.bfloat16)
    normed_b = layer_norm(stream_b, norm_gains[1])
    outgoing = normed_b.reshape(1, frame_count, block_pixels, channels)
    gathered = lax.all_to_all(outgoing, "frame", split_axis=1, concat_axis=0, tiled=True)[:, 0]
    frames, pixels, _ = gathered.shape
    projected_b = jnp.dot(
        gathered.reshape(-1, channels), time_qkv, preferred_element_type=jnp.float32
    ).astype(jnp.bfloat16)
    projected_b = projected_b.reshape(frames, pixels, 3 * channels)
    mixed = time_attend(
        projected_b[..., :channels],
        projected_b[..., channels : 2 * channels],
        projected_b[..., 2 * channels :],
    )
    time_mix = mixed[:, None]
    returned = lax.all_to_all(time_mix, "frame", split_axis=0, concat_axis=1, tiled=True).reshape(
        pixel_count, channels
    )
    stream_c = (
        stream_b.astype(jnp.float32)
        + jnp.dot(returned, time_out, preferred_element_type=jnp.float32)
    ).astype(jnp.bfloat16)
    normed_c = layer_norm(stream_c, norm_gains[2])
    inner_act = jax.nn.gelu(
        jnp.dot(normed_c, mlp_in, preferred_element_type=jnp.float32), approximate=True
    ).astype(jnp.bfloat16)
    result = (
        stream_c.astype(jnp.float32)
        + jnp.dot(inner_act, mlp_out, preferred_element_type=jnp.float32)
    ).astype(jnp.bfloat16)
    return result.reshape(1, 1, rows_here, row_width, channels)


LOG2E = 1.4426950408889634
LANES = 128
PARAMS = pltpu.CompilerParams(vmem_limit_bytes=20 * 1024 * 1024)


def dot(a, b):
    return jnp.dot(a, b, preferred_element_type=jnp.float32)


def dot_dims(a, b, left, right):
    return lax.dot_general(
        a, b, (((left,), (right,)), ((), ())), preferred_element_type=jnp.float32
    )


def row_queries(own_ref, gains_ref, qkv_ref):
    channels = own_ref.shape[1]
    normed = layer_norm(own_ref[...], gains_ref[0:1, :])
    return dot(normed, qkv_ref[:, :channels]).astype(jnp.bfloat16)


def row_keys_values(other_ref, gains_ref, qkv_ref):
    channels = other_ref.shape[1]
    normed = layer_norm(other_ref[...], gains_ref[0:1, :])
    keys = dot(normed, qkv_ref[:, channels : 2 * channels]).astype(jnp.bfloat16)
    values = dot(normed, qkv_ref[:, 2 * channels :]).astype(jnp.bfloat16)
    return keys, values.T


def cross_heads(queries, keys, values, mix_ref):
    length, channels = keys.shape
    head_dim = channels // HEADS
    lane = lax.broadcasted_iota(jnp.int32, (1, LANES), 1)
    ones = jnp.ones((16, length), jnp.bfloat16)

    def head_scores(head):
        tile = head * head_dim // LANES
        low = head * head_dim - tile * LANES
        held = (lane >= low) & (lane < low + head_dim)
        columns = slice(tile * LANES, (tile + 1) * LANES)
        key_part = jnp.where(held, keys[:, columns], jnp.zeros((), jnp.bfloat16))
        return dot_dims(key_part, queries[:, columns], 1, 1)

    ahead = head_scores(0)
    for head in range(HEADS):
        scores = ahead
        if head + 1 < HEADS:
            ahead = head_scores(head + 1)
        top = jnp.max(scores, axis=0, keepdims=True)
        expo = jnp.exp2((scores - top) * (head_dim**-0.5 * LOG2E)).astype(jnp.bfloat16)
        here = slice(head * head_dim, (head + 1) * head_dim)
        mixed = dot(jnp.concatenate([values[here, :], ones], axis=0), expo)
        over = 1.0 / mixed[head_dim : head_dim + 1]
        mix_ref[here, :] = (mixed[:head_dim] * over).astype(jnp.bfloat16)


def after_cross(own, mix_ref, gains_ref, out_ref, time_ref):
    stream = own.astype(jnp.float32) + dot_dims(mix_ref[...], out_ref[...], 0, 0)
    stream = stream.astype(jnp.bfloat16)
    normed = layer_norm(stream, gains_ref[1:2, :])
    return stream, dot_dims(time_ref[...], normed, 0, 1).astype(jnp.bfloat16)


def row_kernel(own_ref, other_ref, gains_ref, qkv_ref, out_ref, time_ref, stream_ref, proj_ref, mix_ref):
    queries = row_queries(own_ref, gains_ref, qkv_ref)
    keys, values = row_keys_values(other_ref, gains_ref, qkv_ref)
    cross_heads(queries, keys, values, mix_ref)
    stream_ref[...], proj_ref[...] = after_cross(
        own_ref[...], mix_ref, gains_ref, out_ref, time_ref
    )


def time_heads(projs, pixels, mixes):
    frames = len(projs)
    channels = mixes[0].shape[0]
    head_dim = channels // HEADS

    def one_head(head, _):
        def rows(ref, part):
            start = pl.multiple_of(part * channels + head * head_dim, head_dim)
            return ref[pl.ds(start, head_dim), pixels].astype(jnp.float32)

        keys = [rows(ref, 1) for ref in projs]
        values = [rows(ref, 2) for ref in projs]
        for f in range(frames):
            query = rows(projs[f], 0)
            scores = [jnp.sum(query * key, axis=0, keepdims=True) for key in keys]
            top = functools.reduce(jnp.maximum, scores)
            expo = [jnp.exp2((s - top) * (head_dim**-0.5 * LOG2E)) for s in scores]
            over = 1.0 / functools.reduce(jnp.add, expo)
            mixed = None
            for g in range(frames):
                share = (expo[g] * over).astype(jnp.bfloat16).astype(jnp.float32)
                part = share * values[g]
                mixed = part if mixed is None else mixed + part
            start = pl.multiple_of(head * head_dim, head_dim)
            mixes[f][pl.ds(start, head_dim), :] = mixed.astype(jnp.bfloat16)
        return 0

    lax.fori_loop(0, HEADS, one_head, 0)


def finish_tail(
    own, mix_ref, first, gains_ref, out_ref, time_ref, time_out_ref, projs, streams, proj_ref, mixes, results
):
    count = own.shape[0]
    stream, proj_ref[...] = after_cross(own, mix_ref, gains_ref, out_ref, time_ref)
    time_heads(
        [ref.at[:, first : first + count] for ref in projs] + [proj_ref], slice(None), mixes
    )
    before = [ref[first : first + count, :] for ref in streams] + [stream]
    for f, result in enumerate(results):
        result[...] = (
            before[f].astype(jnp.float32) + dot_dims(mixes[f][...], time_out_ref[...], 0, 0)
        ).astype(jnp.bfloat16)


def finish_head_kernel(frames, own_ref, other_ref, gains_ref, qkv_ref, out_ref, time_ref, time_out_ref, *refs):
    projs, streams = refs[: frames - 1], refs[frames - 1 : 2 * frames - 2]
    refs = refs[2 * frames - 2 :]
    results, refs = refs[:frames], refs[frames:]
    queries_ref, keys_ref, values_ref, mix_ref, proj_ref = refs[:5]
    count = results[0].shape[0]
    queries = row_queries(own_ref, gains_ref, qkv_ref)
    keys, values = row_keys_values(other_ref, gains_ref, qkv_ref)
    queries_ref[...] = queries[count:]
    keys_ref[...] = keys
    values_ref[...] = values
    cross_heads(queries[:count], keys, values, mix_ref)
    finish_tail(
        own_ref[:count, :], mix_ref, 0, gains_ref, out_ref, time_ref, time_out_ref,
        projs, streams, proj_ref, refs[5:], results,
    )


def finish_rest_kernel(
    frames, own_ref, queries_ref, keys_ref, values_ref, gains_ref, out_ref, time_ref, time_out_ref, *refs
):
    projs, streams = refs[: frames - 1], refs[frames - 1 : 2 * frames - 2]
    refs = refs[2 * frames - 2 :]
    results, refs = refs[:frames], refs[frames:]
    count = results[0].shape[0]
    first = own_ref.shape[0] - count
    cross_heads(queries_ref[...], keys_ref[...], values_ref[...], refs[0])
    finish_tail(
        own_ref[first:, :], refs[0], first, gains_ref, out_ref, time_ref, time_out_ref,
        projs, streams, refs[1], refs[2:], results,
    )


def mlp_kernel(pieces, *refs):
    gains_ref, in_ref, out_ref, result_ref = refs[pieces:]
    first = 0
    for ref in refs[:pieces]:
        stream = ref[...]
        normed = layer_norm(stream, gains_ref[2:3, :])
        inner = jax.nn.gelu(dot(normed, in_ref[...]), approximate=True).astype(jnp.bfloat16)
        result_ref[first : first + stream.shape[0], :] = (
            stream.astype(jnp.float32) + dot(inner, out_ref[...])
        ).astype(jnp.bfloat16)
        first += stream.shape[0]


def array(*shape):
    return jax.ShapeDtypeStruct(shape, jnp.bfloat16)


def attend_row(own, other, norm_gains, cross_qkv, cross_out, time_qkv):
    length, channels = own.shape
    return pl.pallas_call(
        row_kernel,
        out_shape=(array(length, channels), array(3 * channels, length)),
        scratch_shapes=[pltpu.VMEM((channels, length), jnp.bfloat16)],
        compiler_params=PARAMS,
        cost_estimate=pl.CostEstimate(
            flops=2 * length * channels * 7 * channels + 4 * length * length * channels * HEADS,
            bytes_accessed=2 * (6 * length * channels + 7 * channels * channels),
            transcendentals=HEADS * length * length,
        ),
        name="attend_row",
    )(own, other, norm_gains, cross_qkv, cross_out, time_qkv)


def finish_cost(length, count, channels, frames):
    return pl.CostEstimate(
        flops=2 * length * channels * 3 * channels + 4 * length * count * channels * HEADS,
        bytes_accessed=2 * (8 * frames * count * channels + 8 * channels * channels),
        transcendentals=HEADS * length * count,
    )


def finish_scratch(count, channels, frames):
    return (
        [pltpu.VMEM((channels, count), jnp.bfloat16)]
        + [pltpu.VMEM((3 * channels, count), jnp.bfloat16)]
        + [pltpu.VMEM((channels, count), jnp.bfloat16)] * frames
    )


def finish_head(count, own, other, weights, time_out, projs, streams):
    norm_gains, cross_qkv, cross_out, time_qkv = weights
    length, channels = own.shape
    frames = len(projs) + 1
    out = pl.pallas_call(
        functools.partial(finish_head_kernel, frames),
        out_shape=[array(count, channels)] * frames
        + [array(length - count, channels), array(length, channels), array(channels, length)],
        scratch_shapes=finish_scratch(count, channels, frames),
        compiler_params=PARAMS,
        cost_estimate=finish_cost(length, count, channels, frames),
        name="finish_head",
    )(own, other, norm_gains, cross_qkv, cross_out, time_qkv, time_out, *projs, *streams)
    return out[:frames], out[frames:]


def finish_rest(own, kept, weights, time_out, projs, streams):
    norm_gains, _, cross_out, time_qkv = weights
    length, channels = own.shape
    frames = len(projs) + 1
    count = kept[0].shape[0]
    return pl.pallas_call(
        functools.partial(finish_rest_kernel, frames),
        out_shape=[array(count, channels)] * frames,
        scratch_shapes=finish_scratch(count, channels, frames),
        compiler_params=PARAMS,
        cost_estimate=finish_cost(length, count, channels, frames),
        name="finish_rest",
    )(own, *kept, norm_gains, cross_out, time_qkv, time_out, *projs, *streams)


def mlp(pieces, norm_gains, mlp_in, mlp_out):
    channels, hidden = mlp_in.shape
    length = sum(piece.shape[0] for piece in pieces)
    return pl.pallas_call(
        functools.partial(mlp_kernel, len(pieces)),
        out_shape=array(length, channels),
        compiler_params=PARAMS,
        cost_estimate=pl.CostEstimate(
            flops=4 * length * channels * hidden,
            bytes_accessed=4 * (length * channels + channels * hidden),
            transcendentals=length * hidden,
        ),
        name="mlp",
    )(*pieces, norm_gains, mlp_in, mlp_out)


def copy_kernel(after_ref, value_ref, result_ref):
    result_ref[...] = value_ref[...]


def copied_after(after, value):
    return pl.pallas_call(
        copy_kernel,
        out_shape=jax.ShapeDtypeStruct(value.shape, value.dtype),
        in_specs=[pl.BlockSpec(memory_space=pl.ANY), pl.BlockSpec(memory_space=pltpu.VMEM)],
        out_specs=pl.BlockSpec(memory_space=pltpu.VMEM),
        compiler_params=PARAMS,
        cost_estimate=pl.CostEstimate(flops=0, bytes_accessed=0, transcendentals=0),
        name="copied_after",
    )(after, value)


def frame_swapped(value, distance):
    count = lax.axis_size("frame")
    return lax.ppermute(value, "frame", [(i, i ^ distance) for i in range(count)])


def local_rows(feats, norm_gains, cross_qkv, cross_out, time_qkv, time_out, mlp_in, mlp_out):
    rows_here, row_width, _ = feats.shape[2:]
    here = lax.axis_index("frame")
    rows = feats[0, 0]
    weights = (norm_gains, cross_qkv, cross_out, time_qkv)
    order = list(range(1, rows_here))
    own_rows = {0: lax.dynamic_index_in_dim(rows, here, 0, keepdims=False)}
    for d in order:
        piece = lax.dynamic_index_in_dim(rows, here ^ d, 0, keepdims=False)
        own_rows[d] = frame_swapped(piece, d)
    streams, projs = [], []

    def other_view(d):
        return swapped(own_rows[d], "view", 0)

    others = {0: other_view(0)}
    for d in range(len(order)):
        stream, proj = attend_row(own_rows[d], others[d], *weights)
        if d == 0:
            weights = (copied_after(stream, norm_gains),) + weights[1:]
        soon = order[:-1] if d == 0 else order[-1:] if d + 1 == len(order) else []
        if soon:
            *held, stream = lax.optimization_barrier((*(own_rows[e] for e in soon), stream))
            own_rows.update(zip(soon, held))
            others.update((e, other_view(e)) for e in soon)
        streams.append(stream)
        projs.append(proj)
    own, other = own_rows[order[-1]], others[order[-1]]
    count = min(row_width, 2 * LANES)
    early, kept = finish_head(count, own, other, weights, time_out, projs, streams)
    late = finish_rest(own, kept, weights, time_out, projs, streams)
    far = order[1:]
    result = jnp.zeros(rows.shape, jnp.bfloat16)
    arrived = []

    def send(pieces, d, first):
        done = mlp(pieces, norm_gains, mlp_in, mlp_out)
        arrived.append((here ^ d, first, frame_swapped(done, d)))

    for d in far:
        send([early[d]], d, 0)
    for d in far:
        send([late[d]], d, count)
    send([early[1], late[1]], 1, 0)
    own_result = mlp([early[0], late[0]], norm_gains, mlp_in, mlp_out)
    arrived.insert(0, (here, 0, own_result))
    for row, first, value in arrived:
        result = lax.dynamic_update_slice(result, value[None], (row, first, 0))
    return result[None, None]


def local(feats, *rest):
    rows_here = feats.shape[2]
    whole = rows_here == lax.axis_size("frame") and rows_here & (rows_here - 1) == 0
    return (local_rows if whole else local_pixels)(feats, *rest)


def solution(mesh):
    placed = (P(("clips", "view"), "frame", "rows", None, None), P(), P(), P(), P(), P(), P(), P())
    return jax.shard_map(
        local,
        mesh=mesh,
        in_specs=placed,
        out_specs=P(("clips", "view"), "frame", "rows", None, None),
        check_vma=False,
    )
```

```python
import functools

import jax
import jax.numpy as jnp
from jax import lax
from jax.experimental import pallas as pl
from jax.experimental.pallas import tpu as pltpu
from jax.sharding import PartitionSpec as P


HEADS = 8


EPSILON = 1e-05


def swapped(value, axis, bit):
    return lax.ppermute(value, axis, [(i, i ^ 1 << bit) for i in range(lax.axis_size(axis))])


def layer_norm(values, norm_gain):
    wide = values.astype(jnp.float32)
    centre = jnp.mean(wide, axis=-1, keepdims=True)
    spread = jnp.mean((wide - centre) ** 2, axis=-1, keepdims=True)
    return ((wide - centre) * lax.rsqrt(spread + EPSILON) * norm_gain).astype(jnp.bfloat16)


def row_attend(queries, key_rows, value_rows):
    length, channels = queries.shape
    head_dim = channels // HEADS
    q_heads = queries.reshape(length, HEADS, head_dim)
    k_heads = key_rows.reshape(length, HEADS, head_dim)
    v_heads = value_rows.reshape(length, HEADS, head_dim)
    scores = jnp.einsum(
        "qhd,khd->hqk", q_heads, k_heads, preferred_element_type=jnp.float32
    ) * head_dim ** (-0.5)
    top_score = jnp.max(scores, axis=-1, keepdims=True)
    expo = jnp.exp(scores - top_score)
    shares = (expo / jnp.sum(expo, axis=-1, keepdims=True)).astype(jnp.bfloat16)
    mixed = jnp.einsum("hqk,khd->qhd", shares, v_heads, preferred_element_type=jnp.float32)
    return mixed.reshape(length, channels).astype(jnp.bfloat16)


def time_attend(queries, key_rows, value_rows):
    frames, pixels, channels = queries.shape
    head_dim = channels // HEADS
    q_heads = queries.reshape(frames, pixels, HEADS, head_dim)
    k_heads = key_rows.reshape(frames, pixels, HEADS, head_dim)
    v_heads = value_rows.reshape(frames, pixels, HEADS, head_dim)
    scores = jnp.einsum(
        "fnhd,gnhd->hfgn", q_heads, k_heads, preferred_element_type=jnp.float32
    ) * head_dim ** (-0.5)
    top_score = jnp.max(scores, axis=2, keepdims=True)
    expo = jnp.exp(scores - top_score)
    shares = (expo / jnp.sum(expo, axis=2, keepdims=True)).astype(jnp.bfloat16)
    mixed = jnp.einsum("hfgn,gnhd->fnhd", shares, v_heads, preferred_element_type=jnp.float32)
    return mixed.reshape(frames, pixels, channels).astype(jnp.bfloat16)


def local_pixels(feats, norm_gains, cross_qkv, cross_out, time_qkv, time_out, mlp_in, mlp_out):
    rows_here, row_width, channels = (feats.shape[2], feats.shape[3], feats.shape[4])
    frame_count = lax.axis_size("frame")
    tokens_flat = feats[0, 0].reshape(-1, channels)
    pixel_count = tokens_flat.shape[0]
    block_pixels = pixel_count // frame_count
    normed_a = layer_norm(tokens_flat, norm_gains[0])
    projected = jnp.dot(normed_a, cross_qkv, preferred_element_type=jnp.float32).astype(
        jnp.bfloat16
    )
    queries = projected[:, :channels]
    partner = swapped(projected[:, channels:], "view", 0)

    def cross_row(pieces):
        return row_attend(pieces[0], pieces[1][:, :channels], pieces[1][:, channels:])

    cross_mix = lax.map(
        cross_row,
        (
            queries.reshape(rows_here, row_width, channels),
            partner.reshape(rows_here, row_width, 2 * channels),
        ),
    )
    cross_mix = cross_mix.reshape(-1, channels)
    stream_b = (
        tokens_flat.astype(jnp.float32)
        + jnp.dot(cross_mix, cross_out, preferred_element_type=jnp.float32)
    ).astype(jnp.bfloat16)
    normed_b = layer_norm(stream_b, norm_gains[1])
    outgoing = normed_b.reshape(1, frame_count, block_pixels, channels)
    gathered = lax.all_to_all(outgoing, "frame", split_axis=1, concat_axis=0, tiled=True)[:, 0]
    frames, pixels, _ = gathered.shape
    projected_b = jnp.dot(
        gathered.reshape(-1, channels), time_qkv, preferred_element_type=jnp.float32
    ).astype(jnp.bfloat16)
    projected_b = projected_b.reshape(frames, pixels, 3 * channels)
    mixed = time_attend(
        projected_b[..., :channels],
        projected_b[..., channels : 2 * channels],
        projected_b[..., 2 * channels :],
    )
    time_mix = mixed[:, None]
    returned = lax.all_to_all(time_mix, "frame", split_axis=0, concat_axis=1, tiled=True).reshape(
        pixel_count, channels
    )
    stream_c = (
        stream_b.astype(jnp.float32)
        + jnp.dot(returned, time_out, preferred_element_type=jnp.float32)
    ).astype(jnp.bfloat16)
    normed_c = layer_norm(stream_c, norm_gains[2])
    inner_act = jax.nn.gelu(
        jnp.dot(normed_c, mlp_in, preferred_element_type=jnp.float32), approximate=True
    ).astype(jnp.bfloat16)
    result = (
        stream_c.astype(jnp.float32)
        + jnp.dot(inner_act, mlp_out, preferred_element_type=jnp.float32)
    ).astype(jnp.bfloat16)
    return result.reshape(1, 1, rows_here, row_width, channels)


LOG2E = 1.4426950408889634
LANES = 128
PARAMS = pltpu.CompilerParams(vmem_limit_bytes=20 * 1024 * 1024)


def dot(a, b):
    return jnp.dot(a, b, preferred_element_type=jnp.float32)


def dot_dims(a, b, left, right):
    return lax.dot_general(
        a, b, (((left,), (right,)), ((), ())), preferred_element_type=jnp.float32
    )


def row_queries(own_ref, gains_ref, qkv_ref):
    channels = own_ref.shape[1]
    normed = layer_norm(own_ref[...], gains_ref[0:1, :])
    return dot(normed, qkv_ref[:, :channels]).astype(jnp.bfloat16)


def row_keys_values(other_ref, gains_ref, qkv_ref):
    channels = other_ref.shape[1]
    normed = layer_norm(other_ref[...], gains_ref[0:1, :])
    keys = dot(normed, qkv_ref[:, channels : 2 * channels]).astype(jnp.bfloat16)
    values = dot(normed, qkv_ref[:, 2 * channels :]).astype(jnp.bfloat16)
    return keys, values.T


def cross_heads(queries, keys, values, mix_ref):
    length, channels = keys.shape
    head_dim = channels // HEADS
    lane = lax.broadcasted_iota(jnp.int32, (1, LANES), 1)
    ones = jnp.ones((16, length), jnp.bfloat16)

    def head_scores(head):
        tile = head * head_dim // LANES
        low = head * head_dim - tile * LANES
        held = (lane >= low) & (lane < low + head_dim)
        columns = slice(tile * LANES, (tile + 1) * LANES)
        key_part = jnp.where(held, keys[:, columns], jnp.zeros((), jnp.bfloat16))
        return dot_dims(key_part, queries[:, columns], 1, 1)

    ahead = head_scores(0)
    for head in range(HEADS):
        scores = ahead
        if head + 1 < HEADS:
            ahead = head_scores(head + 1)
        top = jnp.max(scores, axis=0, keepdims=True)
        expo = jnp.exp2((scores - top) * (head_dim**-0.5 * LOG2E)).astype(jnp.bfloat16)
        here = slice(head * head_dim, (head + 1) * head_dim)
        mixed = dot(jnp.concatenate([values[here, :], ones], axis=0), expo)
        over = 1.0 / mixed[head_dim : head_dim + 1]
        mix_ref[here, :] = (mixed[:head_dim] * over).astype(jnp.bfloat16)


def after_cross(own, mix_ref, gains_ref, out_ref, time_ref):
    stream = own.astype(jnp.float32) + dot_dims(mix_ref[...], out_ref[...], 0, 0)
    stream = stream.astype(jnp.bfloat16)
    normed = layer_norm(stream, gains_ref[1:2, :])
    return stream, dot_dims(time_ref[...], normed, 0, 1).astype(jnp.bfloat16)


def row_kernel(own_ref, other_ref, gains_ref, qkv_ref, out_ref, time_ref, stream_ref, proj_ref, mix_ref):
    queries = row_queries(own_ref, gains_ref, qkv_ref)
    keys, values = row_keys_values(other_ref, gains_ref, qkv_ref)
    cross_heads(queries, keys, values, mix_ref)
    stream_ref[...], proj_ref[...] = after_cross(
        own_ref[...], mix_ref, gains_ref, out_ref, time_ref
    )


def time_heads(projs, asked, mixes):
    frames = len(projs)
    channels = mixes[0].shape[0]
    head_dim = channels // HEADS

    def one_head(head, _):
        def rows(ref, part):
            start = pl.multiple_of(part * channels + head * head_dim, head_dim)
            return ref[pl.ds(start, head_dim), :].astype(jnp.float32)

        keys = [rows(ref, 1) for ref in projs]
        values = [rows(ref, 2) for ref in projs]
        for mix, f in zip(mixes, asked):
            query = rows(projs[f], 0)
            scores = [jnp.sum(query * key, axis=0, keepdims=True) for key in keys]
            top = functools.reduce(jnp.maximum, scores)
            expo = [jnp.exp2((s - top) * (head_dim**-0.5 * LOG2E)) for s in scores]
            over = 1.0 / functools.reduce(jnp.add, expo)
            mixed = None
            for g in range(frames):
                share = (expo[g] * over).astype(jnp.bfloat16).astype(jnp.float32)
                part = share * values[g]
                mixed = part if mixed is None else mixed + part
            start = pl.multiple_of(head * head_dim, head_dim)
            mix[pl.ds(start, head_dim), :] = mixed.astype(jnp.bfloat16)
        return 0

    lax.fori_loop(0, HEADS, one_head, 0)


def time_part(projs, asked, streams, mixes, time_out_ref, results):
    time_heads(projs, asked, mixes)
    for mix, stream, result in zip(mixes, streams, results):
        result[...] = (
            stream.astype(jnp.float32) + dot_dims(mix[...], time_out_ref[...], 0, 0)
        ).astype(jnp.bfloat16)


def queries_kernel(own_ref, gains_ref, qkv_ref, queries_ref):
    queries_ref[...] = row_queries(own_ref, gains_ref, qkv_ref)


def finish_head_kernel(
    frames, own_ref, other_ref, queries_ref, gains_ref, qkv_ref, out_ref, time_ref, time_out_ref, *refs
):
    projs, streams, refs = refs[: frames - 1], refs[frames - 1 : 2 * frames - 2], refs[2 * frames - 2 :]
    results, refs = refs[: frames - 2], refs[frames - 2 :]
    keys_ref, values_ref, proj_ref, mix_ref = refs[:4]
    count = results[0].shape[0]
    keys, values = row_keys_values(other_ref, gains_ref, qkv_ref)
    keys_ref[...] = keys
    values_ref[...] = values
    cross_heads(queries_ref[:count, :], keys, values, mix_ref)
    stream, proj_ref[...] = after_cross(own_ref[:count, :], mix_ref, gains_ref, out_ref, time_ref)
    time_part(
        [ref.at[:, :count] for ref in projs] + [proj_ref],
        range(2, frames),
        [ref[:count, :] for ref in streams[2:]] + [stream],
        refs[4:],
        time_out_ref,
        results,
    )


def finish_rest_kernel(
    frames, own_ref, queries_ref, keys_ref, values_ref, head_ref, gains_ref, out_ref, time_ref, time_out_ref, *refs
):
    projs, streams, refs = refs[: frames - 1], refs[frames - 1 : 2 * frames - 2], refs[2 * frames - 2 :]
    results, near, refs = refs[:frames], refs[frames : frames + 2], refs[frames + 2 :]
    mix_ref, proj_ref, refs = refs[0], refs[1], refs[2:]
    mixes, near_mixes = refs[:frames], refs[frames:]
    first = near[0].shape[0]
    cross_heads(queries_ref[first:, :], keys_ref[...], values_ref[...], mix_ref)
    stream, proj_ref[...] = after_cross(own_ref[first:, :], mix_ref, gains_ref, out_ref, time_ref)
    time_part(
        [ref.at[:, first:] for ref in projs] + [proj_ref],
        range(frames),
        [ref[first:, :] for ref in streams] + [stream],
        mixes,
        time_out_ref,
        results,
    )
    time_part(
        [ref.at[:, :first] for ref in projs] + [head_ref],
        range(2),
        [ref[:first, :] for ref in streams[:2]],
        near_mixes,
        time_out_ref,
        near,
    )


def mlp_kernel(pieces, *refs):
    gains_ref, in_ref, out_ref, result_ref = refs[pieces:]
    first = 0
    for ref in refs[:pieces]:
        stream = ref[...]
        normed = layer_norm(stream, gains_ref[2:3, :])
        inner = jax.nn.gelu(dot(normed, in_ref[...]), approximate=True).astype(jnp.bfloat16)
        result_ref[first : first + stream.shape[0], :] = (
            stream.astype(jnp.float32) + dot(inner, out_ref[...])
        ).astype(jnp.bfloat16)
        first += stream.shape[0]


def array(*shape):
    return jax.ShapeDtypeStruct(shape, jnp.bfloat16)


def attend_row(own, other, norm_gains, cross_qkv, cross_out, time_qkv):
    length, channels = own.shape
    return pl.pallas_call(
        row_kernel,
        out_shape=(array(length, channels), array(3 * channels, length)),
        scratch_shapes=[pltpu.VMEM((channels, length), jnp.bfloat16)],
        compiler_params=PARAMS,
        cost_estimate=pl.CostEstimate(
            flops=2 * length * channels * 7 * channels + 4 * length * length * channels * HEADS,
            bytes_accessed=2 * (6 * length * channels + 7 * channels * channels),
            transcendentals=HEADS * length * length,
        ),
        name="attend_row",
    )(own, other, norm_gains, cross_qkv, cross_out, time_qkv)


def finish_cost(length, count, channels, frames):
    return pl.CostEstimate(
        flops=2 * length * channels * 3 * channels + 4 * length * count * channels * HEADS,
        bytes_accessed=2 * (8 * frames * count * channels + 8 * channels * channels),
        transcendentals=HEADS * length * count,
    )


def scratch(*shape):
    return pltpu.VMEM(shape, jnp.bfloat16)


def row_queries_call(own, norm_gains, cross_qkv):
    length, channels = own.shape
    return pl.pallas_call(
        queries_kernel,
        out_shape=array(length, channels),
        compiler_params=PARAMS,
        cost_estimate=pl.CostEstimate(
            flops=2 * length * channels * channels,
            bytes_accessed=4 * length * channels + 6 * channels * channels,
            transcendentals=length,
        ),
        name="row_queries",
    )(own, norm_gains, cross_qkv)


def finish_head(count, own, other, queries, weights, time_out, projs, streams):
    length, channels = own.shape
    frames = len(projs) + 1
    out = pl.pallas_call(
        functools.partial(finish_head_kernel, frames),
        out_shape=[array(count, channels)] * (frames - 2)
        + [array(length, channels), array(channels, length), array(3 * channels, count)],
        scratch_shapes=[scratch(channels, count)] * (frames - 1),
        compiler_params=PARAMS,
        cost_estimate=finish_cost(length, count, channels, frames),
        name="finish_head",
    )(own, other, queries, *weights, time_out, *projs, *streams)
    return out[: frames - 2], out[frames - 2 :]


def finish_rest(own, queries, kept, weights, time_out, projs, streams):
    norm_gains, _, cross_out, time_qkv = weights
    length, channels = own.shape
    frames = len(projs) + 1
    first = kept[2].shape[1]
    count = length - first
    out = pl.pallas_call(
        functools.partial(finish_rest_kernel, frames),
        out_shape=[array(count, channels)] * frames + [array(first, channels)] * 2,
        scratch_shapes=[scratch(channels, count), scratch(3 * channels, count)]
        + [scratch(channels, count)] * frames
        + [scratch(channels, first)] * 2,
        compiler_params=PARAMS,
        cost_estimate=finish_cost(length, count, channels, frames),
        name="finish_rest",
    )(own, queries, *kept, norm_gains, cross_out, time_qkv, time_out, *projs, *streams)
    return out[:frames], out[frames:]


def take_kernel(distances, here_ref, rows_ref, *refs):
    taken, sems = refs[:-1], refs[-1]
    copies = [
        pltpu.make_async_copy(rows_ref.at[here_ref[0] ^ d], ref, sems.at[i])
        for i, (d, ref) in enumerate(zip(distances, taken))
    ]
    for copy in copies:
        copy.start()
    for copy in copies:
        copy.wait()


def take_rows(here, rows, distances):
    count = len(distances)
    return pl.pallas_call(
        functools.partial(take_kernel, distances),
        out_shape=[array(*rows.shape[1:])] * count,
        in_specs=[pl.BlockSpec(memory_space=pltpu.SMEM), pl.BlockSpec(memory_space=pltpu.HBM)],
        out_specs=[pl.BlockSpec(memory_space=pltpu.VMEM)] * count,
        scratch_shapes=[pltpu.SemaphoreType.DMA((count,))],
        compiler_params=PARAMS,
        name="take_rows",
    )(here, pltpu.with_memory_space_constraint(rows, pltpu.HBM))


def place_kernel(places, here_ref, *refs):
    pieces = refs[: len(places)]
    result_ref, sems = refs[-2:]
    copies = [
        pltpu.make_async_copy(
            ref, result_ref.at[here_ref[0] ^ d, pl.ds(first, ref.shape[0]), :], sems.at[i]
        )
        for i, ((d, first), ref) in enumerate(zip(places, pieces))
    ]
    for copy in copies:
        copy.start()
    for copy in copies:
        copy.wait()


def place_rows(here, pieces, places, shape, result=None):
    held = [] if result is None else [result]
    anywhere = pl.BlockSpec(memory_space=pl.ANY)
    return pl.pallas_call(
        functools.partial(place_kernel, places),
        out_shape=array(*shape),
        in_specs=[pl.BlockSpec(memory_space=pltpu.SMEM)] + [anywhere] * (len(pieces) + len(held)),
        out_specs=anywhere,
        scratch_shapes=[pltpu.SemaphoreType.DMA((len(pieces),))],
        input_output_aliases={1 + len(pieces): 0} if held else {},
        compiler_params=PARAMS,
        name="place_rows",
    )(here, *pieces, *held)


def mlp(pieces, norm_gains, mlp_in, mlp_out):
    channels, hidden = mlp_in.shape
    length = sum(piece.shape[0] for piece in pieces)
    return pl.pallas_call(
        functools.partial(mlp_kernel, len(pieces)),
        out_shape=array(length, channels),
        compiler_params=PARAMS,
        cost_estimate=pl.CostEstimate(
            flops=4 * length * channels * hidden,
            bytes_accessed=4 * (length * channels + channels * hidden),
            transcendentals=length * hidden,
        ),
        name="mlp",
    )(*pieces, norm_gains, mlp_in, mlp_out)


def frame_swapped(value, distance):
    count = lax.axis_size("frame")
    return lax.ppermute(value, "frame", [(i, i ^ distance) for i in range(count)])


def local_rows(feats, norm_gains, cross_qkv, cross_out, time_qkv, time_out, mlp_in, mlp_out):
    rows_here, row_width, _ = feats.shape[2:]
    here = lax.axis_index("frame").astype(jnp.int32).reshape(1)
    rows = feats[0, 0]
    weights = (norm_gains, cross_qkv, cross_out, time_qkv)
    order = list(range(1, rows_here))
    own_rows = dict(enumerate(take_rows(here, rows, [0] + order)))
    for d in order:
        own_rows[d] = frame_swapped(own_rows[d], d)
    streams, projs = [], []

    def other_view(d):
        return swapped(own_rows[d], "view", 0)

    others = {0: other_view(0)}
    for d in range(len(order)):
        stream, proj = attend_row(own_rows[d], others[d], *weights)
        after = order[d]
        own_rows[after], stream = lax.optimization_barrier((own_rows[after], stream))
        others[after] = other_view(after)
        streams.append(stream)
        projs.append(proj)
    own, other = own_rows[order[-1]], others[order[-1]]
    count = min(row_width, 2 * LANES)
    queries = row_queries_call(own, norm_gains, cross_qkv)
    early, kept = finish_head(count, own, other, queries, weights, time_out, projs, streams)
    late, near = finish_rest(own, queries, kept, weights, time_out, projs, streams)

    def send(pieces, d):
        done = mlp(pieces, norm_gains, mlp_in, mlp_out)
        return frame_swapped(done, d)

    far = order[1:]
    sooner = [send([piece], d) for d, piece in zip(far, early)]
    later = [send([late[d]], d) for d in far]
    later.append(send([near[1], late[1]], 1))
    own_result = mlp([near[0], late[0]], norm_gains, mlp_in, mlp_out)
    result = place_rows(
        here, [own_result] + sooner, [(0, 0)] + [(d, 0) for d in far], rows.shape
    )
    result = place_rows(
        here, later, [(d, count) for d in far] + [(1, 0)], rows.shape, result
    )
    return result[None, None]


def local(feats, *rest):
    rows_here = feats.shape[2]
    whole = rows_here == lax.axis_size("frame") and rows_here & (rows_here - 1) == 0
    return (local_rows if whole else local_pixels)(feats, *rest)


def solution(mesh):
    placed = (P(("clips", "view"), "frame", "rows", None, None), P(), P(), P(), P(), P(), P(), P())
    return jax.shard_map(
        local,
        mesh=mesh,
        in_specs=placed,
        out_specs=P(("clips", "view"), "frame", "rows", None, None),
        check_vma=False,
    )
```

```python
import functools

import jax
import jax.numpy as jnp
from jax import lax
from jax.experimental import pallas as pl
from jax.experimental.pallas import tpu as pltpu
from jax.sharding import PartitionSpec as P


HEADS = 8


EPSILON = 1e-05


def swapped(value, axis, bit):
    return lax.ppermute(value, axis, [(i, i ^ 1 << bit) for i in range(lax.axis_size(axis))])


def layer_norm(values, norm_gain):
    wide = values.astype(jnp.float32)
    centre = jnp.mean(wide, axis=-1, keepdims=True)
    spread = jnp.mean((wide - centre) ** 2, axis=-1, keepdims=True)
    return ((wide - centre) * lax.rsqrt(spread + EPSILON) * norm_gain).astype(jnp.bfloat16)


def row_attend(queries, key_rows, value_rows):
    length, channels = queries.shape
    head_dim = channels // HEADS
    q_heads = queries.reshape(length, HEADS, head_dim)
    k_heads = key_rows.reshape(length, HEADS, head_dim)
    v_heads = value_rows.reshape(length, HEADS, head_dim)
    scores = jnp.einsum(
        "qhd,khd->hqk", q_heads, k_heads, preferred_element_type=jnp.float32
    ) * head_dim ** (-0.5)
    top_score = jnp.max(scores, axis=-1, keepdims=True)
    expo = jnp.exp(scores - top_score)
    shares = (expo / jnp.sum(expo, axis=-1, keepdims=True)).astype(jnp.bfloat16)
    mixed = jnp.einsum("hqk,khd->qhd", shares, v_heads, preferred_element_type=jnp.float32)
    return mixed.reshape(length, channels).astype(jnp.bfloat16)


def time_attend(queries, key_rows, value_rows):
    frames, pixels, channels = queries.shape
    head_dim = channels // HEADS
    q_heads = queries.reshape(frames, pixels, HEADS, head_dim)
    k_heads = key_rows.reshape(frames, pixels, HEADS, head_dim)
    v_heads = value_rows.reshape(frames, pixels, HEADS, head_dim)
    scores = jnp.einsum(
        "fnhd,gnhd->hfgn", q_heads, k_heads, preferred_element_type=jnp.float32
    ) * head_dim ** (-0.5)
    top_score = jnp.max(scores, axis=2, keepdims=True)
    expo = jnp.exp(scores - top_score)
    shares = (expo / jnp.sum(expo, axis=2, keepdims=True)).astype(jnp.bfloat16)
    mixed = jnp.einsum("hfgn,gnhd->fnhd", shares, v_heads, preferred_element_type=jnp.float32)
    return mixed.reshape(frames, pixels, channels).astype(jnp.bfloat16)


def local_pixels(feats, norm_gains, cross_qkv, cross_out, time_qkv, time_out, mlp_in, mlp_out):
    rows_here, row_width, channels = (feats.shape[2], feats.shape[3], feats.shape[4])
    frame_count = lax.axis_size("frame")
    tokens_flat = feats[0, 0].reshape(-1, channels)
    pixel_count = tokens_flat.shape[0]
    block_pixels = pixel_count // frame_count
    normed_a = layer_norm(tokens_flat, norm_gains[0])
    projected = jnp.dot(normed_a, cross_qkv, preferred_element_type=jnp.float32).astype(
        jnp.bfloat16
    )
    queries = projected[:, :channels]
    partner = swapped(projected[:, channels:], "view", 0)

    def cross_row(pieces):
        return row_attend(pieces[0], pieces[1][:, :channels], pieces[1][:, channels:])

    cross_mix = lax.map(
        cross_row,
        (
            queries.reshape(rows_here, row_width, channels),
            partner.reshape(rows_here, row_width, 2 * channels),
        ),
    )
    cross_mix = cross_mix.reshape(-1, channels)
    stream_b = (
        tokens_flat.astype(jnp.float32)
        + jnp.dot(cross_mix, cross_out, preferred_element_type=jnp.float32)
    ).astype(jnp.bfloat16)
    normed_b = layer_norm(stream_b, norm_gains[1])
    outgoing = normed_b.reshape(1, frame_count, block_pixels, channels)
    gathered = lax.all_to_all(outgoing, "frame", split_axis=1, concat_axis=0, tiled=True)[:, 0]
    frames, pixels, _ = gathered.shape
    projected_b = jnp.dot(
        gathered.reshape(-1, channels), time_qkv, preferred_element_type=jnp.float32
    ).astype(jnp.bfloat16)
    projected_b = projected_b.reshape(frames, pixels, 3 * channels)
    mixed = time_attend(
        projected_b[..., :channels],
        projected_b[..., channels : 2 * channels],
        projected_b[..., 2 * channels :],
    )
    time_mix = mixed[:, None]
    returned = lax.all_to_all(time_mix, "frame", split_axis=0, concat_axis=1, tiled=True).reshape(
        pixel_count, channels
    )
    stream_c = (
        stream_b.astype(jnp.float32)
        + jnp.dot(returned, time_out, preferred_element_type=jnp.float32)
    ).astype(jnp.bfloat16)
    normed_c = layer_norm(stream_c, norm_gains[2])
    inner_act = jax.nn.gelu(
        jnp.dot(normed_c, mlp_in, preferred_element_type=jnp.float32), approximate=True
    ).astype(jnp.bfloat16)
    result = (
        stream_c.astype(jnp.float32)
        + jnp.dot(inner_act, mlp_out, preferred_element_type=jnp.float32)
    ).astype(jnp.bfloat16)
    return result.reshape(1, 1, rows_here, row_width, channels)


LOG2E = 1.4426950408889634
LANES = 128
PARAMS = pltpu.CompilerParams(vmem_limit_bytes=20 * 1024 * 1024)


def dot(a, b):
    return jnp.dot(a, b, preferred_element_type=jnp.float32)


def dot_dims(a, b, left, right):
    return lax.dot_general(
        a, b, (((left,), (right,)), ((), ())), preferred_element_type=jnp.float32
    )


def row_queries(own_ref, gains_ref, qkv_ref):
    channels = own_ref.shape[1]
    normed = layer_norm(own_ref[...], gains_ref[0:1, :])
    return dot(normed, qkv_ref[:, :channels]).astype(jnp.bfloat16)


def row_keys_values(other_ref, gains_ref, qkv_ref):
    channels = other_ref.shape[1]
    normed = layer_norm(other_ref[...], gains_ref[0:1, :])
    keys = dot(normed, qkv_ref[:, channels : 2 * channels]).astype(jnp.bfloat16)
    values = dot(normed, qkv_ref[:, 2 * channels :]).astype(jnp.bfloat16)
    return keys, values.T


def cross_heads(queries, keys, values, mix_ref):
    length, channels = keys.shape
    head_dim = channels // HEADS
    lane = lax.broadcasted_iota(jnp.int32, (1, LANES), 1)
    ones = jnp.ones((16, length), jnp.bfloat16)

    def head_scores(head):
        tile = head * head_dim // LANES
        low = head * head_dim - tile * LANES
        held = (lane >= low) & (lane < low + head_dim)
        columns = slice(tile * LANES, (tile + 1) * LANES)
        key_part = jnp.where(held, keys[:, columns], jnp.zeros((), jnp.bfloat16))
        return dot_dims(key_part, queries[:, columns], 1, 1)

    ahead = head_scores(0)
    for head in range(HEADS):
        scores = ahead
        if head + 1 < HEADS:
            ahead = head_scores(head + 1)
        top = jnp.max(scores, axis=0, keepdims=True)
        expo = jnp.exp2((scores - top) * (head_dim**-0.5 * LOG2E)).astype(jnp.bfloat16)
        here = slice(head * head_dim, (head + 1) * head_dim)
        mixed = dot(jnp.concatenate([values[here, :], ones], axis=0), expo)
        over = 1.0 / mixed[head_dim : head_dim + 1]
        mix_ref[here, :] = (mixed[:head_dim] * over).astype(jnp.bfloat16)


def after_cross(own, mix_ref, gains_ref, out_ref, time_ref):
    stream = own.astype(jnp.float32) + dot_dims(mix_ref[...], out_ref[...], 0, 0)
    stream = stream.astype(jnp.bfloat16)
    normed = layer_norm(stream, gains_ref[1:2, :])
    return stream, dot_dims(time_ref[...], normed, 0, 1).astype(jnp.bfloat16)


def row_kernel(
    own_ref, other_ref, queries_ref, gains_ref, qkv_ref, out_ref, time_ref, stream_ref, proj_ref, mix_ref
):
    queries = queries_ref[...]
    keys, values = row_keys_values(other_ref, gains_ref, qkv_ref)
    cross_heads(queries, keys, values, mix_ref)
    stream_ref[...], proj_ref[...] = after_cross(
        own_ref[...], mix_ref, gains_ref, out_ref, time_ref
    )


def time_heads(projs, asked, mixes):
    frames = len(projs)
    channels = mixes[0].shape[0]
    head_dim = channels // HEADS

    def one_head(head, _):
        def rows(ref, part):
            start = pl.multiple_of(part * channels + head * head_dim, head_dim)
            return ref[pl.ds(start, head_dim), :].astype(jnp.float32)

        keys = [rows(ref, 1) for ref in projs]
        values = [rows(ref, 2) for ref in projs]
        for mix, f in zip(mixes, asked):
            query = rows(projs[f], 0)
            scores = [jnp.sum(query * key, axis=0, keepdims=True) for key in keys]
            top = functools.reduce(jnp.maximum, scores)
            expo = [jnp.exp2((s - top) * (head_dim**-0.5 * LOG2E)) for s in scores]
            over = 1.0 / functools.reduce(jnp.add, expo)
            mixed = None
            for g in range(frames):
                share = (expo[g] * over).astype(jnp.bfloat16).astype(jnp.float32)
                part = share * values[g]
                mixed = part if mixed is None else mixed + part
            start = pl.multiple_of(head * head_dim, head_dim)
            mix[pl.ds(start, head_dim), :] = mixed.astype(jnp.bfloat16)
        return 0

    lax.fori_loop(0, HEADS, one_head, 0)


def time_part(projs, asked, streams, mixes, time_out_ref, results):
    time_heads(projs, asked, mixes)
    for mix, stream, result in zip(mixes, streams, results):
        result[...] = (
            stream.astype(jnp.float32) + dot_dims(mix[...], time_out_ref[...], 0, 0)
        ).astype(jnp.bfloat16)


def queries_kernel(own_ref, gains_ref, qkv_ref, queries_ref):
    queries_ref[...] = row_queries(own_ref, gains_ref, qkv_ref)


def finish_head_kernel(
    frames, own_ref, other_ref, queries_ref, gains_ref, qkv_ref, out_ref, time_ref, time_out_ref, *refs
):
    projs, streams, refs = refs[: frames - 1], refs[frames - 1 : 2 * frames - 2], refs[2 * frames - 2 :]
    results, refs = refs[: frames - 2], refs[frames - 2 :]
    keys_ref, values_ref, proj_ref, mix_ref = refs[:4]
    count = results[0].shape[0]
    keys, values = row_keys_values(other_ref, gains_ref, qkv_ref)
    keys_ref[...] = keys
    values_ref[...] = values
    cross_heads(queries_ref[:count, :], keys, values, mix_ref)
    stream, proj_ref[...] = after_cross(own_ref[:count, :], mix_ref, gains_ref, out_ref, time_ref)
    time_part(
        [ref.at[:, :count] for ref in projs] + [proj_ref],
        range(2, frames),
        [ref[:count, :] for ref in streams[2:]] + [stream],
        refs[4:],
        time_out_ref,
        results,
    )


def finish_rest_kernel(
    frames, own_ref, queries_ref, keys_ref, values_ref, head_ref, gains_ref, out_ref, time_ref, time_out_ref, *refs
):
    projs, streams, refs = refs[: frames - 1], refs[frames - 1 : 2 * frames - 2], refs[2 * frames - 2 :]
    results, near, refs = refs[:frames], refs[frames : frames + 2], refs[frames + 2 :]
    mix_ref, proj_ref, refs = refs[0], refs[1], refs[2:]
    mixes, near_mixes = refs[:frames], refs[frames:]
    first = near[0].shape[0]
    cross_heads(queries_ref[first:, :], keys_ref[...], values_ref[...], mix_ref)
    stream, proj_ref[...] = after_cross(own_ref[first:, :], mix_ref, gains_ref, out_ref, time_ref)
    time_part(
        [ref.at[:, first:] for ref in projs] + [proj_ref],
        range(frames),
        [ref[first:, :] for ref in streams] + [stream],
        mixes,
        time_out_ref,
        results,
    )
    time_part(
        [ref.at[:, :first] for ref in projs] + [head_ref],
        range(2),
        [ref[:first, :] for ref in streams[:2]],
        near_mixes,
        time_out_ref,
        near,
    )


def mlp_kernel(pieces, *refs):
    gains_ref, in_ref, out_ref, result_ref = refs[pieces:]
    first = 0
    for ref in refs[:pieces]:
        stream = ref[...]
        normed = layer_norm(stream, gains_ref[2:3, :])
        inner = jax.nn.gelu(dot(normed, in_ref[...]), approximate=True).astype(jnp.bfloat16)
        result_ref[first : first + stream.shape[0], :] = (
            stream.astype(jnp.float32) + dot(inner, out_ref[...])
        ).astype(jnp.bfloat16)
        first += stream.shape[0]


def array(*shape):
    return jax.ShapeDtypeStruct(shape, jnp.bfloat16)


def attend_row(own, other, queries, norm_gains, cross_qkv, cross_out, time_qkv):
    length, channels = own.shape
    return pl.pallas_call(
        row_kernel,
        out_shape=(array(length, channels), array(3 * channels, length)),
        scratch_shapes=[pltpu.VMEM((channels, length), jnp.bfloat16)],
        compiler_params=PARAMS,
        cost_estimate=pl.CostEstimate(
            flops=2 * length * channels * 7 * channels + 4 * length * length * channels * HEADS,
            bytes_accessed=2 * (6 * length * channels + 7 * channels * channels),
            transcendentals=HEADS * length * length,
        ),
        name="attend_row",
    )(own, other, queries, norm_gains, cross_qkv, cross_out, time_qkv)


def finish_cost(length, count, channels, frames):
    return pl.CostEstimate(
        flops=2 * length * channels * 3 * channels + 4 * length * count * channels * HEADS,
        bytes_accessed=2 * (8 * frames * count * channels + 8 * channels * channels),
        transcendentals=HEADS * length * count,
    )


def scratch(*shape):
    return pltpu.VMEM(shape, jnp.bfloat16)


def row_queries_call(own, norm_gains, cross_qkv):
    length, channels = own.shape
    return pl.pallas_call(
        queries_kernel,
        out_shape=array(length, channels),
        compiler_params=PARAMS,
        cost_estimate=pl.CostEstimate(
            flops=2 * length * channels * channels,
            bytes_accessed=4 * length * channels + 6 * channels * channels,
            transcendentals=length,
        ),
        name="row_queries",
    )(own, norm_gains, cross_qkv)


def finish_head(count, own, other, queries, weights, time_out, projs, streams):
    length, channels = own.shape
    frames = len(projs) + 1
    out = pl.pallas_call(
        functools.partial(finish_head_kernel, frames),
        out_shape=[array(count, channels)] * (frames - 2)
        + [array(length, channels), array(channels, length), array(3 * channels, count)],
        scratch_shapes=[scratch(channels, count)] * (frames - 1),
        compiler_params=PARAMS,
        cost_estimate=finish_cost(length, count, channels, frames),
        name="finish_head",
    )(own, other, queries, *weights, time_out, *projs, *streams)
    return out[: frames - 2], out[frames - 2 :]


def finish_rest(own, queries, kept, weights, time_out, projs, streams):
    norm_gains, _, cross_out, time_qkv = weights
    length, channels = own.shape
    frames = len(projs) + 1
    first = kept[2].shape[1]
    count = length - first
    out = pl.pallas_call(
        functools.partial(finish_rest_kernel, frames),
        out_shape=[array(count, channels)] * frames + [array(first, channels)] * 2,
        scratch_shapes=[scratch(channels, count), scratch(3 * channels, count)]
        + [scratch(channels, count)] * frames
        + [scratch(channels, first)] * 2,
        compiler_params=PARAMS,
        cost_estimate=finish_cost(length, count, channels, frames),
        name="finish_rest",
    )(own, queries, *kept, norm_gains, cross_out, time_qkv, time_out, *projs, *streams)
    return out[:frames], out[frames:]


def take_kernel(distances, here_ref, rows_ref, *refs):
    taken, sems = refs[:-1], refs[-1]
    copies = [
        pltpu.make_async_copy(rows_ref.at[here_ref[0] ^ d], ref, sems.at[i])
        for i, (d, ref) in enumerate(zip(distances, taken))
    ]
    for copy in copies:
        copy.start()
    for copy in copies:
        copy.wait()


def take_rows(here, rows, distances):
    count = len(distances)
    return pl.pallas_call(
        functools.partial(take_kernel, distances),
        out_shape=[array(*rows.shape[1:])] * count,
        in_specs=[pl.BlockSpec(memory_space=pltpu.SMEM), pl.BlockSpec(memory_space=pltpu.HBM)],
        out_specs=[pl.BlockSpec(memory_space=pltpu.VMEM)] * count,
        scratch_shapes=[pltpu.SemaphoreType.DMA((count,))],
        compiler_params=PARAMS,
        name="take_rows",
    )(here, pltpu.with_memory_space_constraint(rows, pltpu.HBM))


def place_kernel(places, here_ref, *refs):
    pieces = refs[: len(places)]
    result_ref, sems = refs[-2:]
    copies = [
        pltpu.make_async_copy(
            ref, result_ref.at[here_ref[0] ^ d, pl.ds(first, ref.shape[0]), :], sems.at[i]
        )
        for i, ((d, first), ref) in enumerate(zip(places, pieces))
    ]
    for copy in copies:
        copy.start()
    for copy in copies:
        copy.wait()


def place_rows(here, pieces, places, shape, result=None):
    held = [] if result is None else [result]
    anywhere = pl.BlockSpec(memory_space=pl.ANY)
    return pl.pallas_call(
        functools.partial(place_kernel, places),
        out_shape=array(*shape),
        in_specs=[pl.BlockSpec(memory_space=pltpu.SMEM)] + [anywhere] * (len(pieces) + len(held)),
        out_specs=anywhere,
        scratch_shapes=[pltpu.SemaphoreType.DMA((len(pieces),))],
        input_output_aliases={1 + len(pieces): 0} if held else {},
        compiler_params=PARAMS,
        name="place_rows",
    )(here, *pieces, *held)


def mlp(pieces, norm_gains, mlp_in, mlp_out):
    channels, hidden = mlp_in.shape
    length = sum(piece.shape[0] for piece in pieces)
    return pl.pallas_call(
        functools.partial(mlp_kernel, len(pieces)),
        out_shape=array(length, channels),
        compiler_params=PARAMS,
        cost_estimate=pl.CostEstimate(
            flops=4 * length * channels * hidden,
            bytes_accessed=4 * (length * channels + channels * hidden),
            transcendentals=length * hidden,
        ),
        name="mlp",
    )(*pieces, norm_gains, mlp_in, mlp_out)


def frame_swapped(value, distance):
    count = lax.axis_size("frame")
    return lax.ppermute(value, "frame", [(i, i ^ distance) for i in range(count)])


def local_rows(feats, norm_gains, cross_qkv, cross_out, time_qkv, time_out, mlp_in, mlp_out):
    rows_here, row_width, _ = feats.shape[2:]
    here = lax.axis_index("frame").astype(jnp.int32).reshape(1)
    rows = feats[0, 0]
    weights = (norm_gains, cross_qkv, cross_out, time_qkv)
    order = list(range(1, rows_here))
    own_rows = {}
    for taken in (order[:2], [0] + order[2:]):
        own_rows.update(zip(taken, take_rows(here, rows, taken)))
    for d in order:
        own_rows[d] = frame_swapped(own_rows[d], d)
    streams, projs = [], []

    def other_view(d):
        return swapped(own_rows[d], "view", 0)

    others = {0: other_view(0)}
    for d in range(len(order)):
        queries = row_queries_call(own_rows[d], norm_gains, cross_qkv)
        stream, proj = attend_row(own_rows[d], others[d], queries, *weights)
        after = order[d]
        own_rows[after], stream = lax.optimization_barrier((own_rows[after], stream))
        others[after] = other_view(after)
        streams.append(stream)
        projs.append(proj)
    own, other = own_rows[order[-1]], others[order[-1]]
    count = min(row_width, 2 * LANES)
    queries = row_queries_call(own, norm_gains, cross_qkv)
    early, kept = finish_head(count, own, other, queries, weights, time_out, projs, streams)
    late, near = finish_rest(own, queries, kept, weights, time_out, projs, streams)

    def send(pieces, d):
        done = mlp(pieces, norm_gains, mlp_in, mlp_out)
        return frame_swapped(done, d)

    far = order[:0:-1]
    sooner = [send([early[d - 2]], d) for d in far]
    later = [send([late[d]], d) for d in far]
    later.append(send([near[1], late[1]], 1))
    own_result = mlp([near[0], late[0]], norm_gains, mlp_in, mlp_out)
    result = place_rows(
        here, [own_result] + sooner, [(0, 0)] + [(d, 0) for d in far], rows.shape
    )
    result = place_rows(
        here, later, [(d, count) for d in far] + [(1, 0)], rows.shape, result
    )
    return result[None, None]


def local(feats, *rest):
    rows_here = feats.shape[2]
    whole = rows_here == lax.axis_size("frame") == 4
    return (local_rows if whole else local_pixels)(feats, *rest)


def solution(mesh):
    placed = (P(("clips", "view"), "frame", "rows", None, None), P(), P(), P(), P(), P(), P(), P())
    return jax.shard_map(
        local,
        mesh=mesh,
        in_specs=placed,
        out_specs=P(("clips", "view"), "frame", "rows", None, None),
        check_vma=False,
    )
```

```python
import functools

import jax
import jax.numpy as jnp
from jax import lax
from jax.experimental import pallas as pl
from jax.experimental.pallas import tpu as pltpu
from jax.sharding import PartitionSpec as P


HEADS = 8


EPSILON = 1e-05


def swapped(value, axis, bit):
    return lax.ppermute(value, axis, [(i, i ^ 1 << bit) for i in range(lax.axis_size(axis))])


def layer_norm(values, norm_gain):
    wide = values.astype(jnp.float32)
    centre = jnp.mean(wide, axis=-1, keepdims=True)
    spread = jnp.mean((wide - centre) ** 2, axis=-1, keepdims=True)
    return ((wide - centre) * lax.rsqrt(spread + EPSILON) * norm_gain).astype(jnp.bfloat16)


def row_attend(queries, key_rows, value_rows):
    length, channels = queries.shape
    head_dim = channels // HEADS
    q_heads = queries.reshape(length, HEADS, head_dim)
    k_heads = key_rows.reshape(length, HEADS, head_dim)
    v_heads = value_rows.reshape(length, HEADS, head_dim)
    scores = jnp.einsum(
        "qhd,khd->hqk", q_heads, k_heads, preferred_element_type=jnp.float32
    ) * head_dim ** (-0.5)
    top_score = jnp.max(scores, axis=-1, keepdims=True)
    expo = jnp.exp(scores - top_score)
    shares = (expo / jnp.sum(expo, axis=-1, keepdims=True)).astype(jnp.bfloat16)
    mixed = jnp.einsum("hqk,khd->qhd", shares, v_heads, preferred_element_type=jnp.float32)
    return mixed.reshape(length, channels).astype(jnp.bfloat16)


def time_attend(queries, key_rows, value_rows):
    frames, pixels, channels = queries.shape
    head_dim = channels // HEADS
    q_heads = queries.reshape(frames, pixels, HEADS, head_dim)
    k_heads = key_rows.reshape(frames, pixels, HEADS, head_dim)
    v_heads = value_rows.reshape(frames, pixels, HEADS, head_dim)
    scores = jnp.einsum(
        "fnhd,gnhd->hfgn", q_heads, k_heads, preferred_element_type=jnp.float32
    ) * head_dim ** (-0.5)
    top_score = jnp.max(scores, axis=2, keepdims=True)
    expo = jnp.exp(scores - top_score)
    shares = (expo / jnp.sum(expo, axis=2, keepdims=True)).astype(jnp.bfloat16)
    mixed = jnp.einsum("hfgn,gnhd->fnhd", shares, v_heads, preferred_element_type=jnp.float32)
    return mixed.reshape(frames, pixels, channels).astype(jnp.bfloat16)


def local_pixels(feats, norm_gains, cross_qkv, cross_out, time_qkv, time_out, mlp_in, mlp_out):
    rows_here, row_width, channels = (feats.shape[2], feats.shape[3], feats.shape[4])
    frame_count = lax.axis_size("frame")
    tokens_flat = feats[0, 0].reshape(-1, channels)
    pixel_count = tokens_flat.shape[0]
    block_pixels = pixel_count // frame_count
    normed_a = layer_norm(tokens_flat, norm_gains[0])
    projected = jnp.dot(normed_a, cross_qkv, preferred_element_type=jnp.float32).astype(
        jnp.bfloat16
    )
    queries = projected[:, :channels]
    partner = swapped(projected[:, channels:], "view", 0)

    def cross_row(pieces):
        return row_attend(pieces[0], pieces[1][:, :channels], pieces[1][:, channels:])

    cross_mix = lax.map(
        cross_row,
        (
            queries.reshape(rows_here, row_width, channels),
            partner.reshape(rows_here, row_width, 2 * channels),
        ),
    )
    cross_mix = cross_mix.reshape(-1, channels)
    stream_b = (
        tokens_flat.astype(jnp.float32)
        + jnp.dot(cross_mix, cross_out, preferred_element_type=jnp.float32)
    ).astype(jnp.bfloat16)
    normed_b = layer_norm(stream_b, norm_gains[1])
    outgoing = normed_b.reshape(1, frame_count, block_pixels, channels)
    gathered = lax.all_to_all(outgoing, "frame", split_axis=1, concat_axis=0, tiled=True)[:, 0]
    frames, pixels, _ = gathered.shape
    projected_b = jnp.dot(
        gathered.reshape(-1, channels), time_qkv, preferred_element_type=jnp.float32
    ).astype(jnp.bfloat16)
    projected_b = projected_b.reshape(frames, pixels, 3 * channels)
    mixed = time_attend(
        projected_b[..., :channels],
        projected_b[..., channels : 2 * channels],
        projected_b[..., 2 * channels :],
    )
    time_mix = mixed[:, None]
    returned = lax.all_to_all(time_mix, "frame", split_axis=0, concat_axis=1, tiled=True).reshape(
        pixel_count, channels
    )
    stream_c = (
        stream_b.astype(jnp.float32)
        + jnp.dot(returned, time_out, preferred_element_type=jnp.float32)
    ).astype(jnp.bfloat16)
    normed_c = layer_norm(stream_c, norm_gains[2])
    inner_act = jax.nn.gelu(
        jnp.dot(normed_c, mlp_in, preferred_element_type=jnp.float32), approximate=True
    ).astype(jnp.bfloat16)
    result = (
        stream_c.astype(jnp.float32)
        + jnp.dot(inner_act, mlp_out, preferred_element_type=jnp.float32)
    ).astype(jnp.bfloat16)
    return result.reshape(1, 1, rows_here, row_width, channels)


LOG2E = 1.4426950408889634
LANES = 128
PARAMS = pltpu.CompilerParams(vmem_limit_bytes=20 * 1024 * 1024)


def dot(a, b):
    return jnp.dot(a, b, preferred_element_type=jnp.float32)


def dot_dims(a, b, left, right):
    return lax.dot_general(
        a, b, (((left,), (right,)), ((), ())), preferred_element_type=jnp.float32
    )


def row_queries(own_ref, gains_ref, qkv_ref):
    channels = own_ref.shape[1]
    normed = layer_norm(own_ref[...], gains_ref[0:1, :])
    return dot(normed, qkv_ref[:, :channels]).astype(jnp.bfloat16)


def row_keys_values(other_ref, gains_ref, qkv_ref):
    channels = other_ref.shape[1]
    normed = layer_norm(other_ref[...], gains_ref[0:1, :])
    keys = dot(normed, qkv_ref[:, channels : 2 * channels]).astype(jnp.bfloat16)
    values = dot(normed, qkv_ref[:, 2 * channels :]).astype(jnp.bfloat16)
    return keys, values.T


def cross_heads(queries, keys, values, mix_ref):
    length, channels = keys.shape
    head_dim = channels // HEADS
    lane = lax.broadcasted_iota(jnp.int32, (1, LANES), 1)
    ones = jnp.ones((16, length), jnp.bfloat16)

    def head_scores(head):
        tile = head * head_dim // LANES
        low = head * head_dim - tile * LANES
        held = (lane >= low) & (lane < low + head_dim)
        columns = slice(tile * LANES, (tile + 1) * LANES)
        key_part = jnp.where(held, keys[:, columns], jnp.zeros((), jnp.bfloat16))
        return dot_dims(key_part, queries[:, columns], 1, 1)

    ahead = head_scores(0)
    for head in range(HEADS):
        scores = ahead
        if head + 1 < HEADS:
            ahead = head_scores(head + 1)
        top = jnp.max(scores, axis=0, keepdims=True)
        expo = jnp.exp2((scores - top) * (head_dim**-0.5 * LOG2E)).astype(jnp.bfloat16)
        here = slice(head * head_dim, (head + 1) * head_dim)
        mixed = dot(jnp.concatenate([values[here, :], ones], axis=0), expo)
        over = 1.0 / mixed[head_dim : head_dim + 1]
        mix_ref[here, :] = (mixed[:head_dim] * over).astype(jnp.bfloat16)


def after_cross(own, mix_ref, gains_ref, out_ref, time_ref):
    stream = own.astype(jnp.float32) + dot_dims(mix_ref[...], out_ref[...], 0, 0)
    stream = stream.astype(jnp.bfloat16)
    normed = layer_norm(stream, gains_ref[1:2, :])
    return stream, dot_dims(time_ref[...], normed, 0, 1).astype(jnp.bfloat16)


def row_kernel(
    own_ref, other_ref, queries_ref, gains_ref, qkv_ref, out_ref, time_ref, stream_ref, proj_ref, mix_ref
):
    queries = queries_ref[...]
    keys, values = row_keys_values(other_ref, gains_ref, qkv_ref)
    cross_heads(queries, keys, values, mix_ref)
    stream_ref[...], proj_ref[...] = after_cross(
        own_ref[...], mix_ref, gains_ref, out_ref, time_ref
    )


def time_heads(projs, asked, mixes):
    frames = len(projs)
    channels = mixes[0].shape[0]
    head_dim = channels // HEADS

    def one_head(head, _):
        def rows(ref, part):
            start = pl.multiple_of(part * channels + head * head_dim, head_dim)
            return ref[pl.ds(start, head_dim), :].astype(jnp.float32)

        keys = [rows(ref, 1) for ref in projs]
        values = [rows(ref, 2) for ref in projs]
        for mix, f in zip(mixes, asked):
            query = rows(projs[f], 0)
            scores = [jnp.sum(query * key, axis=0, keepdims=True) for key in keys]
            top = functools.reduce(jnp.maximum, scores)
            expo = [jnp.exp2((s - top) * (head_dim**-0.5 * LOG2E)) for s in scores]
            over = 1.0 / functools.reduce(jnp.add, expo)
            mixed = None
            for g in range(frames):
                share = (expo[g] * over).astype(jnp.bfloat16).astype(jnp.float32)
                part = share * values[g]
                mixed = part if mixed is None else mixed + part
            start = pl.multiple_of(head * head_dim, head_dim)
            mix[pl.ds(start, head_dim), :] = mixed.astype(jnp.bfloat16)
        return 0

    lax.fori_loop(0, HEADS, one_head, 0, unroll=4)


def time_part(projs, asked, streams, mixes, time_out_ref, results):
    time_heads(projs, asked, mixes)
    for mix, stream, result in zip(mixes, streams, results):
        result[...] = (
            stream.astype(jnp.float32) + dot_dims(mix[...], time_out_ref[...], 0, 0)
        ).astype(jnp.bfloat16)


def queries_kernel(own_ref, gains_ref, qkv_ref, queries_ref):
    queries_ref[...] = row_queries(own_ref, gains_ref, qkv_ref)


def finish_head_kernel(
    frames, own_ref, other_ref, queries_ref, gains_ref, qkv_ref, out_ref, time_ref, time_out_ref, *refs
):
    projs, streams, refs = refs[: frames - 1], refs[frames - 1 : 2 * frames - 2], refs[2 * frames - 2 :]
    results, refs = refs[: frames - 2], refs[frames - 2 :]
    keys_ref, values_ref, proj_ref, mix_ref = refs[:4]
    count = results[0].shape[0]
    keys, values = row_keys_values(other_ref, gains_ref, qkv_ref)
    keys_ref[...] = keys
    values_ref[...] = values
    cross_heads(queries_ref[:count, :], keys, values, mix_ref)
    stream, proj_ref[...] = after_cross(own_ref[:count, :], mix_ref, gains_ref, out_ref, time_ref)
    time_part(
        [ref.at[:, :count] for ref in projs] + [proj_ref],
        range(2, frames),
        [ref[:count, :] for ref in streams[2:]] + [stream],
        refs[4:],
        time_out_ref,
        results,
    )


def finish_rest_kernel(
    frames, own_ref, queries_ref, keys_ref, values_ref, head_ref, gains_ref, out_ref, time_ref, time_out_ref, *refs
):
    projs, streams, refs = refs[: frames - 1], refs[frames - 1 : 2 * frames - 2], refs[2 * frames - 2 :]
    results, near, refs = refs[:frames], refs[frames : frames + 2], refs[frames + 2 :]
    mix_ref, proj_ref, refs = refs[0], refs[1], refs[2:]
    mixes, near_mixes = refs[:frames], refs[frames:]
    first = near[0].shape[0]
    cross_heads(queries_ref[first:, :], keys_ref[...], values_ref[...], mix_ref)
    stream, proj_ref[...] = after_cross(own_ref[first:, :], mix_ref, gains_ref, out_ref, time_ref)
    time_part(
        [ref.at[:, first:] for ref in projs] + [proj_ref],
        range(frames),
        [ref[first:, :] for ref in streams] + [stream],
        mixes,
        time_out_ref,
        results,
    )
    time_part(
        [ref.at[:, :first] for ref in projs] + [head_ref],
        range(2),
        [ref[:first, :] for ref in streams[:2]],
        near_mixes,
        time_out_ref,
        near,
    )


def gelu(x):
    half = 0.5 * x
    scale = (2 / 3.141592653589793) ** 0.5
    return half + half * jnp.tanh(x * (scale + (scale * 0.044715) * (x * x)))


def mlp_kernel(pieces, *refs):
    gains_ref, in_ref, out_ref, result_ref = refs[pieces:]
    first = 0
    for ref in refs[:pieces]:
        stream = ref[...]
        normed = layer_norm(stream, gains_ref[2:3, :])
        inner = gelu(dot(normed, in_ref[...])).astype(jnp.bfloat16)
        result_ref[first : first + stream.shape[0], :] = (
            stream.astype(jnp.float32) + dot(inner, out_ref[...])
        ).astype(jnp.bfloat16)
        first += stream.shape[0]


def array(*shape):
    return jax.ShapeDtypeStruct(shape, jnp.bfloat16)


def attend_row(own, other, queries, norm_gains, cross_qkv, cross_out, time_qkv):
    length, channels = own.shape
    return pl.pallas_call(
        row_kernel,
        out_shape=(array(length, channels), array(3 * channels, length)),
        scratch_shapes=[pltpu.VMEM((channels, length), jnp.bfloat16)],
        compiler_params=PARAMS,
        cost_estimate=pl.CostEstimate(
            flops=2 * length * channels * 7 * channels + 4 * length * length * channels * HEADS,
            bytes_accessed=2 * (6 * length * channels + 7 * channels * channels),
            transcendentals=HEADS * length * length,
        ),
        name="attend_row",
    )(own, other, queries, norm_gains, cross_qkv, cross_out, time_qkv)


def finish_cost(length, count, channels, frames):
    return pl.CostEstimate(
        flops=2 * length * channels * 3 * channels + 4 * length * count * channels * HEADS,
        bytes_accessed=2 * (8 * frames * count * channels + 8 * channels * channels),
        transcendentals=HEADS * length * count,
    )


def scratch(*shape):
    return pltpu.VMEM(shape, jnp.bfloat16)


def row_queries_call(own, norm_gains, cross_qkv):
    length, channels = own.shape
    return pl.pallas_call(
        queries_kernel,
        out_shape=array(length, channels),
        compiler_params=PARAMS,
        cost_estimate=pl.CostEstimate(
            flops=2 * length * channels * channels,
            bytes_accessed=4 * length * channels + 6 * channels * channels,
            transcendentals=length,
        ),
        name="row_queries",
    )(own, norm_gains, cross_qkv)


def finish_head(count, own, other, queries, weights, time_out, projs, streams):
    length, channels = own.shape
    frames = len(projs) + 1
    out = pl.pallas_call(
        functools.partial(finish_head_kernel, frames),
        out_shape=[array(count, channels)] * (frames - 2)
        + [array(length, channels), array(channels, length), array(3 * channels, count)],
        scratch_shapes=[scratch(channels, count)] * (frames - 1),
        compiler_params=PARAMS,
        cost_estimate=finish_cost(length, count, channels, frames),
        name="finish_head",
    )(own, other, queries, *weights, time_out, *projs, *streams)
    return out[: frames - 2], out[frames - 2 :]


def finish_rest(own, queries, kept, weights, time_out, projs, streams):
    norm_gains, _, cross_out, time_qkv = weights
    length, channels = own.shape
    frames = len(projs) + 1
    first = kept[2].shape[1]
    count = length - first
    out = pl.pallas_call(
        functools.partial(finish_rest_kernel, frames),
        out_shape=[array(count, channels)] * frames + [array(first, channels)] * 2,
        scratch_shapes=[scratch(channels, count), scratch(3 * channels, count)]
        + [scratch(channels, count)] * frames
        + [scratch(channels, first)] * 2,
        compiler_params=PARAMS,
        cost_estimate=finish_cost(length, count, channels, frames),
        name="finish_rest",
    )(own, queries, *kept, norm_gains, cross_out, time_qkv, time_out, *projs, *streams)
    return out[:frames], out[frames:]


def take_kernel(distances, here_ref, rows_ref, *refs):
    taken, sems = refs[:-1], refs[-1]
    copies = [
        pltpu.make_async_copy(rows_ref.at[here_ref[0] ^ d], ref, sems.at[i])
        for i, (d, ref) in enumerate(zip(distances, taken))
    ]
    for copy in copies:
        copy.start()
    for copy in copies:
        copy.wait()


def take_rows(here, rows, distances):
    count = len(distances)
    return pl.pallas_call(
        functools.partial(take_kernel, distances),
        out_shape=[array(*rows.shape[1:])] * count,
        in_specs=[pl.BlockSpec(memory_space=pltpu.SMEM), pl.BlockSpec(memory_space=pltpu.HBM)],
        out_specs=[pl.BlockSpec(memory_space=pltpu.VMEM)] * count,
        scratch_shapes=[pltpu.SemaphoreType.DMA((count,))],
        compiler_params=PARAMS,
        name="take_rows",
    )(here, pltpu.with_memory_space_constraint(rows, pltpu.HBM))


def place_kernel(places, here_ref, *refs):
    pieces = refs[: len(places)]
    result_ref, sems = refs[-2:]
    copies = [
        pltpu.make_async_copy(
            ref, result_ref.at[here_ref[0] ^ d, pl.ds(first, ref.shape[0]), :], sems.at[i]
        )
        for i, ((d, first), ref) in enumerate(zip(places, pieces))
    ]
    for copy in copies:
        copy.start()
    for copy in copies:
        copy.wait()


def place_rows(here, pieces, places, shape, result=None):
    held = [] if result is None else [result]
    anywhere = pl.BlockSpec(memory_space=pl.ANY)
    return pl.pallas_call(
        functools.partial(place_kernel, places),
        out_shape=array(*shape),
        in_specs=[pl.BlockSpec(memory_space=pltpu.SMEM)] + [anywhere] * (len(pieces) + len(held)),
        out_specs=anywhere,
        scratch_shapes=[pltpu.SemaphoreType.DMA((len(pieces),))],
        input_output_aliases={1 + len(pieces): 0} if held else {},
        compiler_params=PARAMS,
        name="place_rows",
    )(here, *pieces, *held)


def mlp(pieces, norm_gains, mlp_in, mlp_out):
    channels, hidden = mlp_in.shape
    length = sum(piece.shape[0] for piece in pieces)
    return pl.pallas_call(
        functools.partial(mlp_kernel, len(pieces)),
        out_shape=array(length, channels),
        compiler_params=PARAMS,
        cost_estimate=pl.CostEstimate(
            flops=4 * length * channels * hidden,
            bytes_accessed=4 * (length * channels + channels * hidden),
            transcendentals=length * hidden,
        ),
        name="mlp",
    )(*pieces, norm_gains, mlp_in, mlp_out)


def frame_swapped(value, distance):
    count = lax.axis_size("frame")
    return lax.ppermute(value, "frame", [(i, i ^ distance) for i in range(count)])


def local_rows(feats, norm_gains, cross_qkv, cross_out, time_qkv, time_out, mlp_in, mlp_out):
    rows_here, row_width, _ = feats.shape[2:]
    here = lax.axis_index("frame").astype(jnp.int32).reshape(1)
    rows = feats[0, 0]
    weights = (norm_gains, cross_qkv, cross_out, time_qkv)
    order = list(range(1, rows_here))
    own_rows = {}
    for taken in (order[:2], [0] + order[2:]):
        own_rows.update(zip(taken, take_rows(here, rows, taken)))
    for d in order:
        own_rows[d] = frame_swapped(own_rows[d], d)
    streams, projs = [], []

    def other_view(d):
        return swapped(own_rows[d], "view", 0)

    others = {0: other_view(0)}
    for d in range(len(order)):
        queries = row_queries_call(own_rows[d], norm_gains, cross_qkv)
        stream, proj = attend_row(own_rows[d], others[d], queries, *weights)
        after = order[d]
        own_rows[after], stream = lax.optimization_barrier((own_rows[after], stream))
        others[after] = other_view(after)
        streams.append(stream)
        projs.append(proj)
    own, other = own_rows[order[-1]], others[order[-1]]
    count = min(row_width, 2 * LANES)
    queries = row_queries_call(own, norm_gains, cross_qkv)
    early, kept = finish_head(count, own, other, queries, weights, time_out, projs, streams)
    late, near = finish_rest(own, queries, kept, weights, time_out, projs, streams)

    def send(pieces, d):
        done = mlp(pieces, norm_gains, mlp_in, mlp_out)
        return frame_swapped(done, d)

    far = order[:0:-1]
    sooner = [send([early[d - 2]], d) for d in far]
    later = [send([late[d]], d) for d in far]
    later.append(send([near[1], late[1]], 1))
    own_result = mlp([near[0], late[0]], norm_gains, mlp_in, mlp_out)
    result = place_rows(
        here, [own_result] + sooner, [(0, 0)] + [(d, 0) for d in far], rows.shape
    )
    result = place_rows(
        here, later, [(d, count) for d in far] + [(1, 0)], rows.shape, result
    )
    return result[None, None]


def local(feats, *rest):
    rows_here = feats.shape[2]
    whole = rows_here == lax.axis_size("frame") == 4
    return (local_rows if whole else local_pixels)(feats, *rest)


def solution(mesh):
    placed = (P(("clips", "view"), "frame", "rows", None, None), P(), P(), P(), P(), P(), P(), P())
    return jax.shard_map(
        local,
        mesh=mesh,
        in_specs=placed,
        out_specs=P(("clips", "view"), "frame", "rows", None, None),
        check_vma=False,
    )
```
